128 devices in a mesh: row: 8 (over y, core), col: 16 (over z, x).
Axes of the slice: x: 4, y: 4, z: 4, core: 2. Of those that a mesh axis runs over, the one named last changes fastest.
Arguments:
- points: float32 [3, 262144], P(None, ('row', 'col')), as said below
- values: float32 [16, 262144], P(None, ('row', 'col'))
- tile_lists: int32 [3, 6144], P(None, ('row', 'col')), may hold values from 0 to 127, as said below
Outputs:
- solution: float32 [16, 262144], P(None, ('row', 'col'))
- residual: float32 [16, 262144], P(None, ('row', 'col'))
The draws below stay inside these ranges and needn't reach their ends.
Inputs may be any that keep to these rules, and one draw needn't show every extreme that they name: `tile_lists`: on every device the live slots come first and the rest hold 0, 0, 0; a device holds at most 48 live slots and some device holds exactly that many; no unordered pair of blocks is listed twice, in either order. Block pairs whose points can come within the support radius are listed. Coordinates of point blocks that lie in cells of a square lattice of unit cells, 256 points to a block.
All inputs are finite; a program needn't handle non-finite values.
Results may differ from the reference program's by a relative error of at most 0.0003.
Values sent between devices are 32-bit elements; how exact they have to be, the bound alone decides.
A program may use at most 64 MiB of HBM per device.

```python
import jax
import jax.numpy as jnp
from jax import lax

BLK = 256
BPD = 8
NRHS = 16
ITERS = 2
TILES_DEV = 48
NBLK = 1024
NPTS = 262144
N_ROW = 8
N_COL = 16


def split_code(morton):
    cell_x = jnp.zeros_like(morton)
    cell_y = jnp.zeros_like(morton)
    for level in range(12):
        cell_x = cell_x + morton // 4 ** level % 2 * 2 ** level
        cell_y = cell_y + morton // (2 * 4 ** level) % 2 * 2 ** level
    return (cell_x, cell_y)


def join_code(cell_x, cell_y):
    morton = jnp.zeros_like(cell_x)
    for level in range(12):
        morton = morton + cell_x // 2 ** level % 2 * 4 ** level
        morton = morton + cell_y // 2 ** level % 2 * (2 * 4 ** level)
    return morton


def occupied(key):
    cell_total = 2 * NBLK
    shuffled = jax.random.permutation(jax.random.fold_in(key, 11), cell_total)
    return jnp.sort(shuffled[:NBLK]).astype(jnp.int32)


def draw_points(key, part):
    cell_x, cell_y = split_code(occupied(key))
    corner = jnp.stack([cell_x, cell_y, jnp.zeros_like(cell_x)]).astype(jnp.float32)
    jitter = jax.random.uniform(jax.random.fold_in(key, 21), (3, NBLK, BLK), jnp.float32)
    spread = jnp.array([1.0, 1.0, 0.3], jnp.float32)
    lowest = jnp.array([0.0, 0.0, -0.15], jnp.float32)
    placed = corner[:, :, None] + jitter * spread[:, None, None] + lowest[:, None, None]
    return placed.reshape(3, NPTS)


def draw_values(key, part):
    position = jnp.arange(NPTS, dtype=jnp.float32) / NPTS
    field_gain = jnp.exp(jax.random.uniform(jax.random.fold_in(key, 5), (NRHS, 1), jnp.float32, -0.7, 0.7))
    noise = jax.random.normal(jax.random.fold_in(key, 6), (NRHS, NPTS), jnp.float32)
    rising = 0.6 * jnp.power(3.0, position)
    return noise * rising[None, :] * field_gain


def draw_tile_lists(key, part):
    morton = occupied(key)
    cell_total = 2 * NBLK
    devices = N_ROW * N_COL
    row_span = N_COL * BPD
    col_span = N_ROW * BPD
    slot_total = devices * TILES_DEV
    lookup = jnp.full((cell_total,), -1, jnp.int32).at[morton].set(jnp.arange(NBLK, dtype=jnp.int32))
    cell_x, cell_y = split_code(morton)
    step_x = jnp.array([-1, -1, -1, 0, 0, 0, 1, 1, 1], jnp.int32)
    step_y = jnp.array([-1, 0, 1, -1, 0, 1, -1, 0, 1], jnp.int32)
    near_x = cell_x[:, None] + step_x[None, :]
    near_y = cell_y[:, None] + step_y[None, :]
    near_code = join_code(jnp.maximum(near_x, 0), jnp.maximum(near_y, 0))
    inside = (near_x >= 0) & (near_y >= 0) & (near_code < cell_total)
    partner = jnp.where(inside, lookup[jnp.minimum(near_code, cell_total - 1)], -1)
    own_block = jnp.broadcast_to(jnp.arange(NBLK, dtype=jnp.int32)[:, None], (NBLK, 9))
    usable = (partner >= own_block).reshape(-1)
    lower_block = own_block.reshape(-1)
    upper_block = jnp.maximum(partner.reshape(-1), 0)
    flip = jax.random.randint(jax.random.fold_in(key, 51), (NBLK * 9,), 0, 2)
    row_block = jnp.where(flip == 1, upper_block, lower_block)
    col_block = jnp.where(flip == 1, lower_block, upper_block)
    owner = row_block // row_span * N_COL + col_block // BPD % N_COL
    keyed = jnp.where(usable, owner, devices).astype(jnp.int32)
    order = jnp.argsort(keyed, stable=True)
    sorted_key = keyed[order]
    starts = jnp.searchsorted(sorted_key, jnp.arange(devices + 1, dtype=jnp.int32)).astype(jnp.int32)
    rank_in = jnp.arange(sorted_key.shape[0], dtype=jnp.int32) - starts[sorted_key]
    tallies = starts[1:] - starts[:-1]
    row_sorted = row_block[order]
    col_sorted = col_block[order]
    keep = (sorted_key < devices) & (rank_in < TILES_DEV)
    slot = jnp.where(keep, sorted_key * TILES_DEV + rank_in, slot_total)
    lists = jnp.zeros((3, slot_total), jnp.int32)
    lists = lists.at[0, slot].set(row_sorted % row_span, mode='drop')
    lists = lists.at[1, slot].set(col_sorted // row_span * BPD + col_sorted % BPD, mode='drop')
    lists = lists.at[2, slot].set(1, mode='drop')
    chosen = jax.random.randint(jax.random.fold_in(key, 31), (), 0, devices)
    chosen_row = chosen // N_COL
    chosen_col = chosen % N_COL
    taken = jnp.minimum(tallies[chosen], TILES_DEV)
    pool_row = jnp.arange(row_span, dtype=jnp.int32)[:, None]
    pool_col = jnp.arange(col_span, dtype=jnp.int32)[None, :]
    global_row = chosen_row * row_span + pool_row
    global_col = (pool_col // BPD * N_COL + chosen_col) * BPD + pool_col % BPD
    apart_x = jnp.abs(cell_x[global_row] - cell_x[global_col])
    apart_y = jnp.abs(cell_y[global_row] - cell_y[global_col])
    distant = (jnp.maximum(apart_x, apart_y) >= 2) & (global_row < global_col)
    ranking = jax.random.permutation(jax.random.fold_in(key, 41), row_span * col_span).astype(jnp.int32)
    score = jnp.where(distant.reshape(-1), ranking, -1)
    best_score, best_index = lax.top_k(score, TILES_DEV)
    extra_rank = jnp.arange(TILES_DEV, dtype=jnp.int32)
    extra_use = (extra_rank < TILES_DEV - taken) & (best_score >= 0)
    extra_slot = jnp.where(extra_use, chosen * TILES_DEV + taken + extra_rank, slot_total)
    lists = lists.at[0, extra_slot].set(best_index // col_span, mode='drop')
    lists = lists.at[1, extra_slot].set(best_index % col_span, mode='drop')
    lists = lists.at[2, extra_slot].set(1, mode='drop')
    return lists


def setup_inputs(seed: int = 0) -> dict:
    streams_of = jax.random.split(jax.random.key(seed), 4)
    return {
        "points": draw_points(jax.random.fold_in(streams_of[3], 71), 0),
        "values": draw_values(jax.random.fold_in(streams_of[3], 71), 0),
        "tile_lists": draw_tile_lists(jax.random.fold_in(streams_of[3], 71), 0),
    }


support = 0.5
ridge_shift = 1.0

def wendland(left, right):
    offsets = left[:, :, :, None] - right[:, :, None, :]
    distance = jnp.sqrt(lax.optimization_barrier(jnp.sum(offsets * offsets, axis=0)))
    scaled = distance / support
    remain = jnp.maximum(1.0 - scaled, 0.0)
    return remain * remain * remain * remain * (4.0 * scaled + 1.0)

def reference(points, values, tile_lists):
    slot_ids = jnp.arange(tile_lists.shape[1], dtype=jnp.int32)
    device = slot_ids // TILES_DEV
    row_id = device // N_COL
    col_id = device % N_COL
    row_block = row_id * (N_COL * BPD) + tile_lists[0]
    col_block = (tile_lists[1] // BPD * N_COL + col_id) * BPD + tile_lists[1] % BPD
    weight = tile_lists[2].astype(jnp.float32)
    mirror_weight = weight * (row_block != col_block).astype(jnp.float32)
    point_blocks = points.reshape(3, NBLK, BLK)
    group_shape = (N_ROW * N_COL, TILES_DEV)
    groups = (row_block.reshape(group_shape), col_block.reshape(group_shape), weight.reshape(group_shape), mirror_weight.reshape(group_shape))

    def operate(vector):
        blocks = vector.reshape(NRHS, NBLK, BLK)

        def visit_group(result_sum, member_set):
            row_index, col_index, row_weight, col_weight = member_set
            kernel = wendland(point_blocks[:, row_index], point_blocks[:, col_index])
            forward = jnp.einsum('gxy,fgy->fgx', kernel, blocks[:, col_index], precision=lax.Precision.HIGHEST)
            behind = jnp.einsum('gxy,fgx->fgy', kernel, blocks[:, row_index], precision=lax.Precision.HIGHEST)
            result_sum = result_sum.at[:, row_index].add(forward * row_weight[None, :, None])
            result_sum = result_sum.at[:, col_index].add(behind * col_weight[None, :, None])
            return (result_sum, None)
        result_sum, _ = lax.scan(visit_group, jnp.zeros((NRHS, NBLK, BLK), jnp.float32), groups)
        return ridge_shift * vector + result_sum.reshape(NRHS, NPTS)
    solution = jnp.zeros_like(values)
    residual = values
    direction = values
    norm_now = lax.optimization_barrier(jnp.sum(residual * residual, axis=1))
    for iteration in range(ITERS):
        applied = operate(direction)
        step_length = norm_now / lax.optimization_barrier(jnp.sum(direction * applied, axis=1))
        solution = solution + step_length[:, None] * direction
        residual = residual - step_length[:, None] * applied
        norm_next = lax.optimization_barrier(jnp.sum(residual * residual, axis=1))
        direction = residual + (norm_next / norm_now)[:, None] * direction
        norm_now = norm_next
    return (solution, residual)
```

```python
import jax
import jax.numpy as jnp
from jax import lax
from jax.experimental import pallas as pl
from jax.experimental.pallas import tpu as pltpu
from jax.sharding import PartitionSpec as P

BLK = 256
MESH = pl.DeviceIdType.MESH
F32 = jnp.float32
BF16 = jnp.bfloat16
VM = pl.BlockSpec(memory_space=pltpu.VMEM)
SM = pl.BlockSpec(memory_space=pltpu.SMEM)


def position():
    nr, nc = lax.axis_size("row"), lax.axis_size("col")
    return lax.axis_index("row"), lax.axis_index("col"), nr, nc


def barrier():
    r, c, nr, nc = position()
    sem = pltpu.get_barrier_semaphore()
    for o in range(1, nc):
        pl.semaphore_signal(sem, 1, device_id=(r, lax.rem(c + o, nc)), device_id_type=MESH)
    for o in range(1, nr):
        pl.semaphore_signal(sem, 1, device_id=(lax.rem(r + o, nr), c), device_id_type=MESH)
    pl.semaphore_wait(sem, nr + nc - 2)


def remote(src, dst, sems, k, to):
    return pltpu.make_async_remote_copy(
        src_ref=src, dst_ref=dst, send_sem=sems.at[0, k], recv_sem=sems.at[1, k],
        device_id=to, device_id_type=MESH,
    )


class Mover:
    def __init__(self, sems):
        self.sems, self.copies = sems, []

    def send(self, src, dst, to):
        copy = remote(src, dst, self.sems, len(self.copies), to)
        copy.start()
        self.copies.append(copy)
        return copy

    def drain(self):
        for copy in self.copies:
            copy.wait_send()


def plane(half):
    r, c, nr, nc = position()
    z, x = lax.div(c, SIDE), lax.rem(c, SIDE)
    first, second = (z, x) if half == 0 else (x, z)

    def slot(df, dg):
        f, g = lax.rem(first + df, SIDE), lax.rem(second + dg, SIDE)
        return f * SIDE + g if half == 0 else g * SIDE + f

    return slot


def column(dy, dcore):
    r, c, nr, nc = position()
    y, core = lax.div(r, 2), lax.rem(r, 2)
    return lax.rem(y + dy, SIDE) * 2 + lax.rem(core + dcore, 2)


HALF = 8
SIDE = 4
WAYS = ((1, 3, 0), (3, 1, 1))


def spread(src, by_row, by_col, sems):
    r, c, nr, nc = position()
    mover = Mover(sems)
    owned = src.shape[1]
    part = owned // 2
    row_to = lambda slot: (r, slot)
    col_to = lambda slot: (slot, c)

    def cell(half, slot, side=None):
        rows = pl.ds(half * HALF, HALF)
        if side is None:
            return by_row.at[slot, rows, :]
        return by_row.at[slot, rows, pl.ds(side * part, part)]

    slots = [plane(0), plane(1)]
    near, far, cross, away = {}, {}, {}, {}
    own = [src.at[pl.ds(half * HALF, HALF), :] for half in (0, 1)]
    for half in (0, 1):
        at = slots[half]
        for go, come, side in WAYS:
            near[half, side] = mover.send(own[half], cell(half, at(0, 0)), row_to(at(go, 0)))
    ring, pair = {}, []
    for go, come, side in WAYS:
        ring[side] = mover.send(src, by_col.at[r], col_to(column(go, 0)))
    pair.append(mover.send(src, by_col.at[r], col_to(column(0, 1))))
    for half in (0, 1):
        at = slots[half]
        for go, come, side in WAYS:
            cross[half, 0, side] = mover.send(own[half], cell(half, at(0, 0)), row_to(at(0, go)))
    yield
    for half in (0, 1):
        at = slots[half]
        for go, come, side in WAYS:
            near[half, side].wait_recv()
            from_slot = at(come, 0)
            far[half, side] = mover.send(
                cell(half, from_slot, side), cell(half, from_slot, side), row_to(at(go, 0))
            )
    for half in (0, 1):
        at = slots[half]
        for _, come, _ in WAYS:
            from_slot = at(come, 0)
            for go, _, side in WAYS:
                cross[half, come, side] = mover.send(
                    cell(half, from_slot), cell(half, from_slot), row_to(at(0, go))
                )
    yield
    further = {}
    for go, come, side in WAYS:
        ring[side].wait_recv()
        rows = pl.ds(side * HALF, HALF)
        from_slot = column(come, 0)
        further[side] = mover.send(
            by_col.at[from_slot, rows, :], by_col.at[from_slot, rows, :], col_to(column(go, 0))
        )
    for _, come, _ in WAYS:
        from_slot = column(come, 0)
        pair.append(mover.send(by_col.at[from_slot], by_col.at[from_slot], col_to(column(0, 1))))

    def pass_on(half, df):
        at = slots[half]
        for go, come, side in WAYS:
            cross[half, df, side].wait_recv()
            from_slot = at(df, come)
            away[half, df, side] = mover.send(
                cell(half, from_slot, side), cell(half, from_slot, side), row_to(at(0, go))
            )

    for half in (0, 1):
        pass_on(half, 0)
    yield
    for half in (0, 1):
        at = slots[half]
        for side in (0, 1):
            far[half, side].wait_recv()
        from_slot = at(2, 0)
        for go, _, side in WAYS:
            cross[half, 2, side] = mover.send(
                cell(half, from_slot), cell(half, from_slot), row_to(at(0, go))
            )
    for side in (0, 1):
        further[side].wait_recv()
    from_slot = column(2, 0)
    pair.append(mover.send(by_col.at[from_slot], by_col.at[from_slot], col_to(column(0, 1))))
    yield
    for df in (3, 1):
        for half in (0, 1):
            pass_on(half, df)
        yield
    for half in (0, 1):
        pass_on(half, 2)
    yield
    for df in (0, 3, 1, 2):
        for half in (0, 1):
            for side in (0, 1):
                away[half, df, side].wait_recv()
    for copy in pair:
        copy.wait_recv()
    mover.drain()


def collect(src_row, src_col, out, land, hold, sems):
    r, c, nr, nc = position()
    mover = Mover(sems)
    row_a, row_b, row_c, row_d, col_a, col_b, col_c = land
    row_t, row_q, row_u, col_q, col_t = hold
    owned = out.shape[1]
    part = owned // 2
    row_to = lambda slot: (r, slot)
    col_to = lambda slot: (slot, c)
    slots = [plane(0), plane(1)]
    lane = lambda side: pl.ds(side * part, part)
    rows = lambda half: pl.ds(half * HALF, HALF)
    first, second, third, fourth = {}, {}, {}, {}
    order = (2, 1, 3, 0)

    pair = []
    for k, dy in enumerate(order):
        pair.append(mover.send(src_col.at[column(dy, 1)], col_a.at[k], col_to(column(0, 1))))
    for k, df in enumerate(order):
        for half in (0, 1):
            at = slots[half]
            for go, come, side in WAYS:
                first[half, k, side] = mover.send(
                    src_row.at[at(df, 2), rows(half), lane(side)], row_a.at[half, k, side],
                    row_to(at(0, go)),
                )
    for k, df in enumerate(order):
        for half in (0, 1):
            at = slots[half]
            for go, come, side in WAYS:
                first[half, k, side].wait_recv()
                keep, other = src_row[at(df, go), rows(half), lane(side)], 1 - side
                row_t[half, k, side, :, lane(side)] = keep + row_a[half, k, side]
                row_t[half, k, side, :, lane(other)] = src_row[at(df, go), rows(half), lane(other)]
                second[half, k, side] = mover.send(
                    row_t.at[half, k, side], row_b.at[half, k, side], row_to(at(0, go))
                )

    for k, dy in enumerate(order):
        pair[k].wait_recv()
        col_q[k] = src_col[column(dy, 0)] + col_a[k]
        if k == 0:
            ring = {}
            for go, come, side in WAYS:
                ring[side] = mover.send(
                    col_q.at[0, rows(side), :], col_b.at[side], col_to(column(go, 0))
                )

    def join(half, k, df):
        at = slots[half]
        for side in (0, 1):
            second[half, k, side].wait_recv()
        row_q[half, k] = (
            src_row[at(df, 0), rows(half), :] + row_b[half, k, 0] + row_b[half, k, 1]
        )

    for half in (0, 1):
        join(half, 0, 2)
        at = slots[half]
        for go, come, side in WAYS:
            third[half, side] = mover.send(
                row_q.at[half, 0, :, lane(side)], row_c.at[half, side], row_to(at(go, 0))
            )
    further = {}
    for go, come, side in WAYS:
        k = order.index(go)
        ring[side].wait_recv()
        other = 1 - side
        col_t[side, rows(side), :] = col_q[k, rows(side), :] + col_b[side]
        col_t[side, rows(other), :] = col_q[k, rows(other), :]
        further[side] = mover.send(col_t.at[side], col_c.at[side], col_to(column(go, 0)))
    for k, df in ((1, 1), (2, 3)):
        for half in (0, 1):
            join(half, k, df)
    for half in (0, 1):
        at = slots[half]
        for go, come, side in WAYS:
            k, other = order.index(go), 1 - side
            third[half, side].wait_recv()
            row_u[half, side, :, lane(side)] = row_q[half, k, :, lane(side)] + row_c[half, side]
            row_u[half, side, :, lane(other)] = row_q[half, k, :, lane(other)]
            fourth[half, side] = mover.send(
                row_u.at[half, side], row_d.at[half, side], row_to(at(go, 0))
            )
    for half in (0, 1):
        join(half, 3, 0)
    for side in (0, 1):
        further[side].wait_recv()
    total = col_q[3] + col_c[0] + col_c[1]
    for half in (0, 1):
        for side in (0, 1):
            fourth[half, side].wait_recv()
        out[rows(half), :] = (
            total[half * HALF:(half + 1) * HALF] + row_q[half, 3] + row_d[half, 0] + row_d[half, 1]
        )
    mover.drain()


def finish(copies):
    for copy in copies:
        copy.wait()


def lanes(x):
    total = x[:, 0:128]
    for k in range(1, x.shape[1] // 128):
        total = total + x[:, k * 128:(k + 1) * 128]
    return total


def reduce_row(mine, land, sems, base):
    r, c, nr, nc = position()
    copies = []
    for o in range(1, nc):
        copies.append(remote(mine, land.at[o - 1], sems, base + o - 1, (r, lax.rem(c + o, nc))))
    for copy in copies:
        copy.start()
    return copies


def reduce_col(mine, land, sems, base):
    r, c, nr, nc = position()
    copies = []
    for o in range(1, nr):
        copies.append(remote(mine, land.at[o - 1], sems, base + o - 1, (lax.rem(r + o, nr), c)))
    for copy in copies:
        copy.start()
    return copies


def total_of(mine, land, n):
    total = mine[...]
    for o in range(n):
        total = total + land[o]
    return total


def tiles_kernel(lists, pts, v, khi, klo, vr, vc, own, pr, pc, psem, vsem):
    r, c, nr, nc = position()
    held = own.shape[0]
    for b in range(held):
        block = pts[:, b * BLK:(b + 1) * BLK]
        own[b] = block
        pr[c * held + b] = block
        pc[r * held + b] = block
    vr[c] = v[...]
    vc[r] = v[...]
    barrier()
    early = []
    for o in range(1, nc):
        to = pr.at[pl.ds(c * held, held)]
        early.append(remote(own, to, psem, len(early), (r, lax.rem(c + o, nc))))
    for o in range(1, nr):
        to = pc.at[pl.ds(r * held, held)]
        early.append(remote(own, to, psem, len(early), (lax.rem(r + o, nr), c)))
    for copy in early:
        copy.start()
    late = spread(v, vr, vc, vsem)
    next(late)
    finish(early)

    def tile(s, _):
        left = pr[lists[0, s]]
        right = pc[lists[1, s]]
        down = jnp.transpose(left)
        for k in range(0, BLK, 32):
            square = None
            for x in range(3):
                offset = down[k:k + 32, x:x + 1] - right[x:x + 1, :]
                square = offset * offset if square is None else square + offset * offset
            scaled = 2.0 * (square * lax.rsqrt(jnp.maximum(square, 1e-30)))
            remain = jnp.maximum(1.0 - scaled, 0.0)
            remain = remain * remain
            value = remain * remain * (4.0 * scaled + 1.0)
            high = value.astype(BF16)
            khi[s, k:k + 32, :] = high
            klo[s, k:k + 32, :] = (value - high.astype(F32)).astype(BF16)
        return 0

    slots, pauses = lists.shape[1], 7
    for k in range(pauses):
        lax.fori_loop(slots * k // pauses, slots * (k + 1) // pauses, tile, 0)
        next(late, None)


def split(x):
    high = x.astype(BF16)
    low = (x - high.astype(F32)).astype(BF16)
    return high, low


def contract(x, khi, klo, dims):
    n = x.shape[0]
    high, low = split(x)
    both = jnp.concatenate([high, low], axis=0)
    first = lax.dot_general(both, khi, (dims, ((), ())), preferred_element_type=F32)
    second = lax.dot_general(high, klo, (dims, ((), ())), preferred_element_type=F32)
    return first[:n] + first[n:] + second


def apply_kernel(lists, khi, klo, vr, vc, sr, sc):
    r, c, nr, nc = position()
    sr[...] = jnp.zeros_like(sr)
    sc[...] = jnp.zeros_like(sc)
    slots = lists.shape[1]
    live = lax.fori_loop(0, slots, lambda s, n: n + lists[2, s], 0)

    def visit(s, _):
        i, j = lists[0, s], lists[1, s]
        di, dj = lax.shift_right_logical(i, 3), lax.shift_right_logical(j, 3)
        bi = pl.ds(pl.multiple_of((i & 7) * BLK, BLK), BLK)
        bj = pl.ds(pl.multiple_of((j & 7) * BLK, BLK), BLK)
        same = jnp.logical_and(jnp.logical_and(di == c, dj == r), (i & 7) == (j & 7))
        mirror = jnp.where(same, 0.0, 1.0).astype(F32)
        high, low = khi[s], klo[s]
        sr[di, :, bi] += contract(vc[dj, :, bj], high, low, ((1,), (1,)))
        sc[dj, :, bj] += mirror * contract(vr[di, :, bi], high, low, ((1,), (0,)))
        return 0

    lax.fori_loop(0, live, visit, 0)


def merge_kernel(d, sr, sc, w, vr, vc, dots, sums, *rest):
    land, hold = rest[:7], rest[7:12]
    mine, land_a, land_b, csem, vsem, dsem = rest[12:]
    r, c, nr, nc = position()
    barrier()
    collect(sr, sc, sums, land, hold, csem)
    image = d[...] + sums[...]
    w[...] = image
    vr[c] = image
    vc[r] = image
    mine[0, 0] = lanes(d[...] * d[...])
    mine[0, 1] = lanes(d[...] * image)
    late = spread(w, vr, vc, vsem)
    next(late)
    first = reduce_row(mine.at[0], land_a, dsem, 0)
    for _ in range(3):
        next(late)
    finish(first)
    mine[1] = total_of(mine.at[0], land_a, nc - 1)
    second = reduce_col(mine.at[1], land_b, dsem, nc - 1)
    for _ in late:
        pass
    finish(second)
    dots[...] = total_of(mine.at[1], land_b, nr - 1)


def final_kernel(d, w, sr, sc, dots, x, res, sums, *rest):
    land, hold = rest[:7], rest[7:12]
    mine, land_a, land_b, csem, dsem = rest[12:]
    r, c, nr, nc = position()
    norm = jnp.sum(dots[0], axis=1, keepdims=True)
    step = norm / jnp.sum(dots[1], axis=1, keepdims=True)
    residual = d[...] - step * w[...]
    mine[0] = lanes(residual * residual)
    barrier()
    first = reduce_row(mine.at[0], land_a, dsem, 0)
    collect(sr, sc, sums, land, hold, csem)
    finish(first)
    mine[1] = total_of(mine.at[0], land_a, nc - 1)
    second = reduce_col(mine.at[1], land_b, dsem, nc - 1)
    finish(second)
    fresh = jnp.sum(total_of(mine.at[1], land_b, nr - 1), axis=1, keepdims=True)
    growth = fresh / norm
    image = w[...] + sums[...]
    direction = residual + growth * d[...]
    applied = w[...] - step * image + growth * w[...]
    mine[2] = lanes(direction * applied)
    third = reduce_row(mine.at[2], land_a.at[pl.ds(nc - 1, nc - 1)], dsem, nc + nr - 2)
    finish(third)
    total = mine[2]
    for o in range(nc - 1):
        total = total + land_a[nc - 1 + o]
    mine[3] = total
    fourth = reduce_col(mine.at[3], land_b.at[pl.ds(nr - 1, nr - 1)], dsem, 2 * nc + nr - 3)
    finish(fourth)
    for o in range(nr - 1):
        total = total + land_b[nr - 1 + o]
    stride = fresh / jnp.sum(total, axis=1, keepdims=True)
    x[...] = step * d[...] + stride * direction
    res[...] = residual - stride * applied


def params(cid=None):
    if cid is None:
        return pltpu.CompilerParams(vmem_limit_bytes=24000 * 1024)
    return pltpu.CompilerParams(collective_id=cid, has_side_effects=True, vmem_limit_bytes=24000 * 1024)


def shape(*dims, dtype=F32):
    return jax.ShapeDtypeStruct(dims, dtype)


def local(points, values, tile_lists):
    nr, nc = lax.axis_size("row"), lax.axis_size("col")
    fields, owned = values.shape
    slots = tile_lists.shape[1]
    peers = nr + nc - 2
    sem = lambda n: pltpu.SemaphoreType.DMA((2, n))
    rows, cols = shape(nc, fields, owned), shape(nr, fields, owned)
    tile = shape(slots, BLK, BLK, dtype=BF16)
    part = owned // 2
    landing = [
        pltpu.VMEM((fields, owned), F32),
        pltpu.VMEM((2, SIDE, 2, HALF, part), F32),
        pltpu.VMEM((2, SIDE, 2, HALF, owned), F32),
        pltpu.VMEM((2, 2, HALF, part), F32),
        pltpu.VMEM((2, 2, HALF, owned), F32),
        pltpu.VMEM((SIDE, fields, owned), F32),
        pltpu.VMEM((2, HALF, owned), F32),
        pltpu.VMEM((2, fields, owned), F32),
        pltpu.VMEM((2, SIDE, 2, HALF, owned), F32),
        pltpu.VMEM((2, SIDE, HALF, owned), F32),
        pltpu.VMEM((2, 2, HALF, owned), F32),
        pltpu.VMEM((SIDE, fields, owned), F32),
        pltpu.VMEM((2, fields, owned), F32),
    ]
    ways = 48

    khi, klo, vr, vc = pl.pallas_call(
        tiles_kernel,
        out_shape=(tile, tile, rows, cols),
        in_specs=[SM, VM, VM],
        out_specs=[VM] * 4,
        scratch_shapes=[
            pltpu.VMEM((owned // BLK, 3, BLK), F32),
            pltpu.VMEM((nc * owned // BLK, 3, BLK), F32),
            pltpu.VMEM((nr * owned // BLK, 3, BLK), F32),
            sem(peers), sem(ways),
        ],
        compiler_params=params(0),
        name="gather_and_tiles",
    )(tile_lists, points, values)

    apply = pl.pallas_call(
        apply_kernel,
        out_shape=(rows, cols),
        in_specs=[SM, VM, VM, VM, VM],
        out_specs=[VM] * 2,
        compiler_params=params(),
        name="apply_tiles",
    )
    sr, sc = apply(tile_lists, khi, klo, vr, vc)

    w, wr, wc, dots = pl.pallas_call(
        merge_kernel,
        out_shape=(shape(fields, owned), rows, cols, shape(2, fields, 128)),
        in_specs=[VM] * 3,
        out_specs=[VM] * 4,
        scratch_shapes=landing + [
            pltpu.VMEM((2, 2, fields, 128), F32),
            pltpu.VMEM((nc - 1, 2, fields, 128), F32),
            pltpu.VMEM((nr - 1, 2, fields, 128), F32),
            sem(ways), sem(ways), sem(peers),
        ],
        compiler_params=params(1),
        name="reduce_and_gather",
    )(values, sr, sc)

    sr, sc = apply(tile_lists, khi, klo, wr, wc)

    x, res = pl.pallas_call(
        final_kernel,
        out_shape=(shape(fields, owned), shape(fields, owned)),
        in_specs=[VM] * 5,
        out_specs=[VM] * 2,
        scratch_shapes=landing + [
            pltpu.VMEM((4, fields, 128), F32),
            pltpu.VMEM((2 * (nc - 1), fields, 128), F32),
            pltpu.VMEM((2 * (nr - 1), fields, 128), F32),
            sem(ways), sem(2 * peers),
        ],
        compiler_params=params(2),
        name="reduce_and_finish",
    )(values, w, sr, sc, dots)
    return x, res


def solution(mesh):
    placed = P(None, ("row", "col"))
    return jax.shard_map(
        local, mesh=mesh, in_specs=(placed,) * 3, out_specs=(placed, placed), check_vma=False
    )
```

```python
import jax
import jax.numpy as jnp
from jax import lax
from jax.experimental import pallas as pl
from jax.experimental.pallas import tpu as pltpu
from jax.sharding import PartitionSpec as P

BLK = 256
MESH = pl.DeviceIdType.MESH
F32 = jnp.float32
BF16 = jnp.bfloat16
VM = pl.BlockSpec(memory_space=pltpu.VMEM)
SM = pl.BlockSpec(memory_space=pltpu.SMEM)


def position():
    nr, nc = lax.axis_size("row"), lax.axis_size("col")
    return lax.axis_index("row"), lax.axis_index("col"), nr, nc


def barrier():
    r, c, nr, nc = position()
    sem = pltpu.get_barrier_semaphore()
    for o in range(1, nc):
        pl.semaphore_signal(sem, 1, device_id=(r, lax.rem(c + o, nc)), device_id_type=MESH)
    for o in range(1, nr):
        pl.semaphore_signal(sem, 1, device_id=(lax.rem(r + o, nr), c), device_id_type=MESH)
    pl.semaphore_wait(sem, nr + nc - 2)


def remote(src, dst, sems, k, to):
    return pltpu.make_async_remote_copy(
        src_ref=src, dst_ref=dst, send_sem=sems.at[0, k], recv_sem=sems.at[1, k],
        device_id=to, device_id_type=MESH,
    )


class Mover:
    def __init__(self, sems):
        self.sems, self.copies = sems, []

    def send(self, src, dst, to):
        copy = remote(src, dst, self.sems, len(self.copies), to)
        copy.start()
        self.copies.append(copy)
        return copy

    def drain(self):
        for copy in self.copies:
            copy.wait_send()


def plane(half):
    r, c, nr, nc = position()
    z, x = lax.div(c, SIDE), lax.rem(c, SIDE)
    first, second = (z, x) if half == 0 else (x, z)

    def slot(df, dg):
        f, g = lax.rem(first + df, SIDE), lax.rem(second + dg, SIDE)
        return f * SIDE + g if half == 0 else g * SIDE + f

    return slot


def column(dy, dcore):
    r, c, nr, nc = position()
    y, core = lax.div(r, 2), lax.rem(r, 2)
    return lax.rem(y + dy, SIDE) * 2 + lax.rem(core + dcore, 2)


HALF = 8
SIDE = 4
WAYS = ((1, 3, 0), (3, 1, 1))


def spread(src, by_row, by_col, sems):
    r, c, nr, nc = position()
    mover = Mover(sems)
    owned = src.shape[1]
    part = owned // 2
    row_to = lambda slot: (r, slot)
    col_to = lambda slot: (slot, c)

    def cell(half, slot, side=None):
        rows = pl.ds(half * HALF, HALF)
        if side is None:
            return by_row.at[slot, rows, :]
        return by_row.at[slot, rows, pl.ds(side * part, part)]

    slots = [plane(0), plane(1)]
    near, far, cross, away = {}, {}, {}, {}
    own = [src.at[pl.ds(half * HALF, HALF), :] for half in (0, 1)]
    for half in (0, 1):
        at = slots[half]
        for go, come, side in WAYS:
            near[half, side] = mover.send(own[half], cell(half, at(0, 0)), row_to(at(go, 0)))
    ring, pair = {}, []
    for go, come, side in WAYS:
        ring[side] = mover.send(src, by_col.at[r], col_to(column(go, 0)))
    pair.append(mover.send(src, by_col.at[r], col_to(column(0, 1))))
    for half in (0, 1):
        at = slots[half]
        for go, come, side in WAYS:
            cross[half, 0, side] = mover.send(own[half], cell(half, at(0, 0)), row_to(at(0, go)))
    yield
    for half in (0, 1):
        at = slots[half]
        for go, come, side in WAYS:
            near[half, side].wait_recv()
            from_slot = at(come, 0)
            far[half, side] = mover.send(
                cell(half, from_slot, side), cell(half, from_slot, side), row_to(at(go, 0))
            )
    for half in (0, 1):
        at = slots[half]
        for _, come, _ in WAYS:
            from_slot = at(come, 0)
            for go, _, side in WAYS:
                cross[half, come, side] = mover.send(
                    cell(half, from_slot), cell(half, from_slot), row_to(at(0, go))
                )
    yield
    further = {}
    for go, come, side in WAYS:
        ring[side].wait_recv()
        rows = pl.ds(side * HALF, HALF)
        from_slot = column(come, 0)
        further[side] = mover.send(
            by_col.at[from_slot, rows, :], by_col.at[from_slot, rows, :], col_to(column(go, 0))
        )
    for _, come, _ in WAYS:
        from_slot = column(come, 0)
        pair.append(mover.send(by_col.at[from_slot], by_col.at[from_slot], col_to(column(0, 1))))

    def pass_on(half, df):
        at = slots[half]
        for go, come, side in WAYS:
            cross[half, df, side].wait_recv()
            from_slot = at(df, come)
            away[half, df, side] = mover.send(
                cell(half, from_slot, side), cell(half, from_slot, side), row_to(at(0, go))
            )

    for half in (0, 1):
        pass_on(half, 0)
    yield
    for half in (0, 1):
        at = slots[half]
        for side in (0, 1):
            far[half, side].wait_recv()
        from_slot = at(2, 0)
        for go, _, side in WAYS:
            cross[half, 2, side] = mover.send(
                cell(half, from_slot), cell(half, from_slot), row_to(at(0, go))
            )
    for side in (0, 1):
        further[side].wait_recv()
    from_slot = column(2, 0)
    pair.append(mover.send(by_col.at[from_slot], by_col.at[from_slot], col_to(column(0, 1))))
    yield
    for df in (3, 1):
        for half in (0, 1):
            pass_on(half, df)
        yield
    for half in (0, 1):
        pass_on(half, 2)
    yield
    for df in (0, 3, 1, 2):
        for half in (0, 1):
            for side in (0, 1):
                away[half, df, side].wait_recv()
    for copy in pair:
        copy.wait_recv()
    mover.drain()


def collect(src_row, src_col, out, land, hold, sems):
    r, c, nr, nc = position()
    mover = Mover(sems)
    row_a, row_b, row_c, row_d, col_a, col_b, col_c = land
    row_t, row_q, row_u, col_q, col_t = hold
    owned = out.shape[1]
    part = owned // 2
    row_to = lambda slot: (r, slot)
    col_to = lambda slot: (slot, c)
    slots = [plane(0), plane(1)]
    lane = lambda side: pl.ds(side * part, part)
    rows = lambda half: pl.ds(half * HALF, HALF)
    first, second, third, fourth = {}, {}, {}, {}
    order = (2, 1, 3, 0)

    pair = []
    for k, dy in enumerate(order):
        pair.append(mover.send(src_col.at[column(dy, 1)], col_a.at[k], col_to(column(0, 1))))
    for k, df in enumerate(order):
        for half in (0, 1):
            at = slots[half]
            for go, come, side in WAYS:
                first[half, k, side] = mover.send(
                    src_row.at[at(df, 2), rows(half), lane(side)], row_a.at[half, k, side],
                    row_to(at(0, go)),
                )
    yield
    for k, df in enumerate(order):
        for half in (0, 1):
            at = slots[half]
            for go, come, side in WAYS:
                first[half, k, side].wait_recv()
                keep, other = src_row[at(df, go), rows(half), lane(side)], 1 - side
                row_t[half, k, side, :, lane(side)] = keep + row_a[half, k, side]
                row_t[half, k, side, :, lane(other)] = src_row[at(df, go), rows(half), lane(other)]
                second[half, k, side] = mover.send(
                    row_t.at[half, k, side], row_b.at[half, k, side], row_to(at(0, go))
                )

    for k, dy in enumerate(order):
        pair[k].wait_recv()
        col_q[k] = src_col[column(dy, 0)] + col_a[k]
        if k == 0:
            ring = {}
            for go, come, side in WAYS:
                ring[side] = mover.send(
                    col_q.at[0, rows(side), :], col_b.at[side], col_to(column(go, 0))
                )

    def join(half, k, df):
        at = slots[half]
        for side in (0, 1):
            second[half, k, side].wait_recv()
        row_q[half, k] = (
            src_row[at(df, 0), rows(half), :] + row_b[half, k, 0] + row_b[half, k, 1]
        )

    for half in (0, 1):
        join(half, 0, 2)
        at = slots[half]
        for go, come, side in WAYS:
            third[half, side] = mover.send(
                row_q.at[half, 0, :, lane(side)], row_c.at[half, side], row_to(at(go, 0))
            )
    yield
    further = {}
    for go, come, side in WAYS:
        k = order.index(go)
        ring[side].wait_recv()
        other = 1 - side
        col_t[side, rows(side), :] = col_q[k, rows(side), :] + col_b[side]
        col_t[side, rows(other), :] = col_q[k, rows(other), :]
        further[side] = mover.send(col_t.at[side], col_c.at[side], col_to(column(go, 0)))
    for k, df in ((1, 1), (2, 3)):
        for half in (0, 1):
            join(half, k, df)
    for half in (0, 1):
        at = slots[half]
        for go, come, side in WAYS:
            k, other = order.index(go), 1 - side
            third[half, side].wait_recv()
            row_u[half, side, :, lane(side)] = row_q[half, k, :, lane(side)] + row_c[half, side]
            row_u[half, side, :, lane(other)] = row_q[half, k, :, lane(other)]
            fourth[half, side] = mover.send(
                row_u.at[half, side], row_d.at[half, side], row_to(at(go, 0))
            )
    yield
    for half in (0, 1):
        join(half, 3, 0)
    for side in (0, 1):
        further[side].wait_recv()
    total = col_q[3] + col_c[0] + col_c[1]
    for half in (0, 1):
        for side in (0, 1):
            fourth[half, side].wait_recv()
        out[rows(half), :] = (
            total[half * HALF:(half + 1) * HALF] + row_q[half, 3] + row_d[half, 0] + row_d[half, 1]
        )
    mover.drain()


def finish(copies):
    for copy in copies:
        copy.wait()


def lanes(x):
    total = x[:, 0:128]
    for k in range(1, x.shape[1] // 128):
        total = total + x[:, k * 128:(k + 1) * 128]
    return total


def reduce_row(mine, land, sems, base):
    r, c, nr, nc = position()
    copies = []
    for o in range(1, nc):
        copies.append(remote(mine, land.at[o - 1], sems, base + o - 1, (r, lax.rem(c + o, nc))))
    for copy in copies:
        copy.start()
    return copies


def reduce_col(mine, land, sems, base):
    r, c, nr, nc = position()
    copies = []
    for o in range(1, nr):
        copies.append(remote(mine, land.at[o - 1], sems, base + o - 1, (lax.rem(r + o, nr), c)))
    for copy in copies:
        copy.start()
    return copies


def total_of(mine, land, n):
    total = mine[...]
    for o in range(n):
        total = total + land[o]
    return total


def tiles_kernel(lists, pts, v, khi, klo, vr, vc, own, pr, pc, psem, vsem):
    r, c, nr, nc = position()
    held = own.shape[0]
    for b in range(held):
        block = pts[:, b * BLK:(b + 1) * BLK]
        own[b] = block
        pr[c * held + b] = block
        pc[r * held + b] = block
    vr[c] = v[...]
    vc[r] = v[...]
    barrier()
    early = []
    for o in range(1, nc):
        to = pr.at[pl.ds(c * held, held)]
        early.append(remote(own, to, psem, len(early), (r, lax.rem(c + o, nc))))
    for o in range(1, nr):
        to = pc.at[pl.ds(r * held, held)]
        early.append(remote(own, to, psem, len(early), (lax.rem(r + o, nr), c)))
    for copy in early:
        copy.start()
    late = spread(v, vr, vc, vsem)
    next(late)
    finish(early)

    def tile(s, _):
        left = pr[lists[0, s]]
        right = pc[lists[1, s]]
        down = jnp.transpose(left)
        for k in range(0, BLK, 32):
            square = None
            for x in range(3):
                offset = down[k:k + 32, x:x + 1] - right[x:x + 1, :]
                square = offset * offset if square is None else square + offset * offset
            scaled = 2.0 * (square * lax.rsqrt(jnp.maximum(square, 1e-30)))
            remain = jnp.maximum(1.0 - scaled, 0.0)
            remain = remain * remain
            value = remain * remain * (4.0 * scaled + 1.0)
            high = value.astype(BF16)
            khi[s, k:k + 32, :] = high
            klo[s, k:k + 32, :] = (value - high.astype(F32)).astype(BF16)
        return 0

    slots, pauses = lists.shape[1], 7
    for k in range(pauses):
        lax.fori_loop(slots * k // pauses, slots * (k + 1) // pauses, tile, 0)
        next(late, None)


def split(x):
    high = x.astype(BF16)
    low = (x - high.astype(F32)).astype(BF16)
    return high, low


def contract(x, khi, klo, dims):
    n = x.shape[0]
    high, low = split(x)
    both = jnp.concatenate([high, low], axis=0)
    first = lax.dot_general(both, khi, (dims, ((), ())), preferred_element_type=F32)
    second = lax.dot_general(high, klo, (dims, ((), ())), preferred_element_type=F32)
    return first[:n] + first[n:] + second


def apply_kernel(lists, khi, klo, vr, vc, sr, sc):
    r, c, nr, nc = position()
    sr[...] = jnp.zeros_like(sr)
    sc[...] = jnp.zeros_like(sc)
    slots = lists.shape[1]
    live = lax.fori_loop(0, slots, lambda s, n: n + lists[2, s], 0)

    def visit(s, _):
        i, j = lists[0, s], lists[1, s]
        di, dj = lax.shift_right_logical(i, 3), lax.shift_right_logical(j, 3)
        bi = pl.ds(pl.multiple_of((i & 7) * BLK, BLK), BLK)
        bj = pl.ds(pl.multiple_of((j & 7) * BLK, BLK), BLK)
        same = jnp.logical_and(jnp.logical_and(di == c, dj == r), (i & 7) == (j & 7))
        mirror = jnp.where(same, 0.0, 1.0).astype(F32)
        high, low = khi[s], klo[s]
        sr[di, :, bi] += contract(vc[dj, :, bj], high, low, ((1,), (1,)))
        sc[dj, :, bj] += mirror * contract(vr[di, :, bi], high, low, ((1,), (0,)))
        return 0

    lax.fori_loop(0, live, visit, 0)


def merge_kernel(d, sr, sc, w, vr, vc, dots, sums, *rest):
    land, hold = rest[:7], rest[7:12]
    mine, land_a, land_b, csem, vsem, dsem = rest[12:]
    r, c, nr, nc = position()
    barrier()
    for _ in collect(sr, sc, sums, land, hold, csem):
        pass
    image = d[...] + sums[...]
    w[...] = image
    vr[c] = image
    vc[r] = image
    mine[0, 0] = lanes(d[...] * d[...])
    mine[0, 1] = lanes(d[...] * image)
    late = spread(w, vr, vc, vsem)
    next(late)
    first = reduce_row(mine.at[0], land_a, dsem, 0)
    for _ in range(3):
        next(late)
    finish(first)
    mine[1] = total_of(mine.at[0], land_a, nc - 1)
    second = reduce_col(mine.at[1], land_b, dsem, nc - 1)
    for _ in late:
        pass
    finish(second)
    dots[...] = total_of(mine.at[1], land_b, nr - 1)


def local_dots(sr, sc, vr, vc, wr, wc, step):
    fields = sr.shape[1]
    size = 256

    def over(part, dirs, images, n, carry):
        pieces = part.shape[2] // size

        def body(k, carry):
            with_residual, with_direction = carry
            for p in range(pieces):
                cut = slice(p * size, (p + 1) * size)
                direction, image = dirs[k, :, cut], images[k, :, cut]
                product = part[k, :, cut]
                with_residual = with_residual + lanes(product * (direction - step * image))
                with_direction = with_direction + lanes(product * direction)
            return with_residual, with_direction

        return lax.fori_loop(0, n, body, carry)

    zero = jnp.zeros((fields, 128), F32)
    carry = over(sr, vr, wr, sr.shape[0], (zero, zero))
    return over(sc, vc, wc, sc.shape[0], carry)


def final_kernel(d, w, sr, sc, dots, vr, vc, wr, wc, x, res, sums, *rest):
    land, hold = rest[:7], rest[7:12]
    mine, land_a, land_b, csem, dsem = rest[12:]
    r, c, nr, nc = position()
    norm = jnp.sum(dots[0], axis=1, keepdims=True)
    cross = jnp.sum(dots[1], axis=1, keepdims=True)
    step = norm / cross
    residual = d[...] - step * w[...]
    barrier()
    parts = collect(sr, sc, sums, land, hold, csem)
    next(parts)
    with_residual, with_direction = local_dots(sr, sc, vr, vc, wr, wc, step)
    along = lanes(residual * w[...])
    mine[0, 0] = lanes(residual * residual)
    mine[0, 1] = along - step * (along + with_residual)
    mine[0, 2] = along - step * with_direction
    first = reduce_row(mine.at[0], land_a, dsem, 0)
    next(parts)
    finish(first)
    mine[1] = total_of(mine.at[0], land_a, nc - 1)
    second = reduce_col(mine.at[1], land_b, dsem, nc - 1)
    for _ in parts:
        pass
    finish(second)
    totals = total_of(mine.at[1], land_b, nr - 1)
    fresh = jnp.sum(totals[0], axis=1, keepdims=True)
    growth = fresh / norm
    square = jnp.sum(totals[1], axis=1, keepdims=True)
    mixed = jnp.sum(totals[2], axis=1, keepdims=True) + (cross - step * cross)
    stride = fresh / (square + growth * mixed + growth * growth * cross)
    image = w[...] + sums[...]
    direction = residual + growth * d[...]
    applied = w[...] - step * image + growth * w[...]
    x[...] = step * d[...] + stride * direction
    res[...] = residual - stride * applied


def params(cid=None):
    if cid is None:
        return pltpu.CompilerParams(vmem_limit_bytes=24000 * 1024)
    return pltpu.CompilerParams(collective_id=cid, has_side_effects=True, vmem_limit_bytes=24000 * 1024)


def shape(*dims, dtype=F32):
    return jax.ShapeDtypeStruct(dims, dtype)


def local(points, values, tile_lists):
    nr, nc = lax.axis_size("row"), lax.axis_size("col")
    fields, owned = values.shape
    slots = tile_lists.shape[1]
    peers = nr + nc - 2
    sem = lambda n: pltpu.SemaphoreType.DMA((2, n))
    rows, cols = shape(nc, fields, owned), shape(nr, fields, owned)
    tile = shape(slots, BLK, BLK, dtype=BF16)
    part = owned // 2
    landing = [
        pltpu.VMEM((fields, owned), F32),
        pltpu.VMEM((2, SIDE, 2, HALF, part), F32),
        pltpu.VMEM((2, SIDE, 2, HALF, owned), F32),
        pltpu.VMEM((2, 2, HALF, part), F32),
        pltpu.VMEM((2, 2, HALF, owned), F32),
        pltpu.VMEM((SIDE, fields, owned), F32),
        pltpu.VMEM((2, HALF, owned), F32),
        pltpu.VMEM((2, fields, owned), F32),
        pltpu.VMEM((2, SIDE, 2, HALF, owned), F32),
        pltpu.VMEM((2, SIDE, HALF, owned), F32),
        pltpu.VMEM((2, 2, HALF, owned), F32),
        pltpu.VMEM((SIDE, fields, owned), F32),
        pltpu.VMEM((2, fields, owned), F32),
    ]
    ways = 48

    khi, klo, vr, vc = pl.pallas_call(
        tiles_kernel,
        out_shape=(tile, tile, rows, cols),
        in_specs=[SM, VM, VM],
        out_specs=[VM] * 4,
        scratch_shapes=[
            pltpu.VMEM((owned // BLK, 3, BLK), F32),
            pltpu.VMEM((nc * owned // BLK, 3, BLK), F32),
            pltpu.VMEM((nr * owned // BLK, 3, BLK), F32),
            sem(peers), sem(ways),
        ],
        compiler_params=params(0),
        name="gather_and_tiles",
    )(tile_lists, points, values)

    apply = pl.pallas_call(
        apply_kernel,
        out_shape=(rows, cols),
        in_specs=[SM, VM, VM, VM, VM],
        out_specs=[VM] * 2,
        compiler_params=params(),
        name="apply_tiles",
    )
    sr, sc = apply(tile_lists, khi, klo, vr, vc)

    w, wr, wc, dots = pl.pallas_call(
        merge_kernel,
        out_shape=(shape(fields, owned), rows, cols, shape(2, fields, 128)),
        in_specs=[VM] * 3,
        out_specs=[VM] * 4,
        scratch_shapes=landing + [
            pltpu.VMEM((2, 2, fields, 128), F32),
            pltpu.VMEM((nc - 1, 2, fields, 128), F32),
            pltpu.VMEM((nr - 1, 2, fields, 128), F32),
            sem(ways), sem(ways), sem(peers),
        ],
        compiler_params=params(1),
        name="reduce_and_gather",
    )(values, sr, sc)

    sr, sc = apply(tile_lists, khi, klo, wr, wc)

    x, res = pl.pallas_call(
        final_kernel,
        out_shape=(shape(fields, owned), shape(fields, owned)),
        in_specs=[VM] * 9,
        out_specs=[VM] * 2,
        scratch_shapes=landing + [
            pltpu.VMEM((2, 3, fields, 128), F32),
            pltpu.VMEM((nc - 1, 3, fields, 128), F32),
            pltpu.VMEM((nr - 1, 3, fields, 128), F32),
            sem(ways), sem(peers),
        ],
        compiler_params=params(2),
        name="reduce_and_finish",
    )(values, w, sr, sc, dots, vr, vc, wr, wc)
    return x, res


def solution(mesh):
    placed = P(None, ("row", "col"))
    return jax.shard_map(
        local, mesh=mesh, in_specs=(placed,) * 3, out_specs=(placed, placed), check_vma=False
    )
```

```python
import jax
import jax.numpy as jnp
from jax import lax
from jax.experimental import pallas as pl
from jax.experimental.pallas import tpu as pltpu
from jax.sharding import PartitionSpec as P

BLK = 256
MESH = pl.DeviceIdType.MESH
F32 = jnp.float32
BF16 = jnp.bfloat16
VM = pl.BlockSpec(memory_space=pltpu.VMEM)
SM = pl.BlockSpec(memory_space=pltpu.SMEM)


def position():
    nr, nc = lax.axis_size("row"), lax.axis_size("col")
    return lax.axis_index("row"), lax.axis_index("col"), nr, nc


def barrier():
    r, c, nr, nc = position()
    sem = pltpu.get_barrier_semaphore()
    for o in range(1, nc):
        pl.semaphore_signal(sem, 1, device_id=(r, lax.rem(c + o, nc)), device_id_type=MESH)
    for o in range(1, nr):
        pl.semaphore_signal(sem, 1, device_id=(lax.rem(r + o, nr), c), device_id_type=MESH)
    pl.semaphore_wait(sem, nr + nc - 2)


def remote(src, dst, sems, k, to):
    return pltpu.make_async_remote_copy(
        src_ref=src, dst_ref=dst, send_sem=sems.at[0, k], recv_sem=sems.at[1, k],
        device_id=to, device_id_type=MESH,
    )


class Mover:
    def __init__(self, sems):
        self.sems, self.copies = sems, []

    def send(self, src, dst, to):
        copy = remote(src, dst, self.sems, len(self.copies), to)
        copy.start()
        self.copies.append(copy)
        return copy

    def drain(self):
        for copy in self.copies:
            copy.wait_send()


def plane(half):
    r, c, nr, nc = position()
    z, x = lax.div(c, SIDE), lax.rem(c, SIDE)
    first, second = (z, x) if half == 0 else (x, z)

    def slot(df, dg):
        f, g = lax.rem(first + df, SIDE), lax.rem(second + dg, SIDE)
        return f * SIDE + g if half == 0 else g * SIDE + f

    return slot


def column(dy, dcore):
    r, c, nr, nc = position()
    y, core = lax.div(r, 2), lax.rem(r, 2)
    return lax.rem(y + dy, SIDE) * 2 + lax.rem(core + dcore, 2)


HALF = 8
SIDE = 4
WAYS = ((1, 3, 0), (3, 1, 1))


def spread(src, by_row, by_col, sems):
    r, c, nr, nc = position()
    mover = Mover(sems)
    owned = src.shape[1]
    part = owned // 2
    row_to = lambda slot: (r, slot)
    col_to = lambda slot: (slot, c)

    def cell(half, slot, side=None):
        rows = pl.ds(half * HALF, HALF)
        if side is None:
            return by_row.at[slot, rows, :]
        return by_row.at[slot, rows, pl.ds(side * part, part)]

    slots = [plane(0), plane(1)]
    near, far, cross, away = {}, {}, {}, {}
    own = [src.at[pl.ds(half * HALF, HALF), :] for half in (0, 1)]
    for half in (0, 1):
        at = slots[half]
        for go, come, side in WAYS:
            near[half, side] = mover.send(own[half], cell(half, at(0, 0)), row_to(at(go, 0)))
    ring, pair = {}, []
    for go, come, side in WAYS:
        ring[side] = mover.send(src, by_col.at[r], col_to(column(go, 0)))
    pair.append(mover.send(src, by_col.at[r], col_to(column(0, 1))))
    for half in (0, 1):
        at = slots[half]
        for go, come, side in WAYS:
            cross[half, 0, side] = mover.send(own[half], cell(half, at(0, 0)), row_to(at(0, go)))
    yield
    for half in (0, 1):
        at = slots[half]
        for go, come, side in WAYS:
            near[half, side].wait_recv()
            from_slot = at(come, 0)
            far[half, side] = mover.send(
                cell(half, from_slot, side), cell(half, from_slot, side), row_to(at(go, 0))
            )
    for half in (0, 1):
        at = slots[half]
        for _, come, _ in WAYS:
            from_slot = at(come, 0)
            for go, _, side in WAYS:
                cross[half, come, side] = mover.send(
                    cell(half, from_slot), cell(half, from_slot), row_to(at(0, go))
                )
    yield
    further = {}
    for go, come, side in WAYS:
        ring[side].wait_recv()
        rows = pl.ds(side * HALF, HALF)
        from_slot = column(come, 0)
        further[side] = mover.send(
            by_col.at[from_slot, rows, :], by_col.at[from_slot, rows, :], col_to(column(go, 0))
        )
    for _, come, _ in WAYS:
        from_slot = column(come, 0)
        pair.append(mover.send(by_col.at[from_slot], by_col.at[from_slot], col_to(column(0, 1))))

    def pass_on(half, df):
        at = slots[half]
        for go, come, side in WAYS:
            cross[half, df, side].wait_recv()
            from_slot = at(df, come)
            away[half, df, side] = mover.send(
                cell(half, from_slot, side), cell(half, from_slot, side), row_to(at(0, go))
            )

    for half in (0, 1):
        pass_on(half, 0)
    yield
    for half in (0, 1):
        at = slots[half]
        for side in (0, 1):
            far[half, side].wait_recv()
        from_slot = at(2, 0)
        for go, _, side in WAYS:
            cross[half, 2, side] = mover.send(
                cell(half, from_slot), cell(half, from_slot), row_to(at(0, go))
            )
    for side in (0, 1):
        further[side].wait_recv()
    from_slot = column(2, 0)
    pair.append(mover.send(by_col.at[from_slot], by_col.at[from_slot], col_to(column(0, 1))))
    yield
    for df in (3, 1):
        for half in (0, 1):
            pass_on(half, df)
        yield
    for half in (0, 1):
        pass_on(half, 2)
    yield
    for df in (0, 3, 1, 2):
        for half in (0, 1):
            for side in (0, 1):
                away[half, df, side].wait_recv()
    for copy in pair:
        copy.wait_recv()
    mover.drain()


def collect(src_row, src_col, out, land, hold, sems):
    r, c, nr, nc = position()
    mover = Mover(sems)
    row_a, row_b, row_c, row_d, col_a, col_b, col_c = land
    row_t, row_q, row_u, col_q, col_t = hold
    owned = out.shape[1]
    part = owned // 2
    row_to = lambda slot: (r, slot)
    col_to = lambda slot: (slot, c)
    slots = [plane(0), plane(1)]
    lane = lambda side: pl.ds(side * part, part)
    rows = lambda half: pl.ds(half * HALF, HALF)
    first, second, third, fourth = {}, {}, {}, {}
    order = (2, 1, 3, 0)

    pair = []
    for k, dy in enumerate(order):
        pair.append(mover.send(src_col.at[column(dy, 1)], col_a.at[k], col_to(column(0, 1))))
    for k, df in enumerate(order):
        for half in (0, 1):
            at = slots[half]
            for go, come, side in WAYS:
                first[half, k, side] = mover.send(
                    src_row.at[at(df, 2), rows(half), lane(side)], row_a.at[half, k, side],
                    row_to(at(0, go)),
                )
    yield
    for k, df in enumerate(order):
        for half in (0, 1):
            at = slots[half]
            for go, come, side in WAYS:
                first[half, k, side].wait_recv()
                keep, other = src_row[at(df, go), rows(half), lane(side)], 1 - side
                row_t[half, k, side, :, lane(side)] = keep + row_a[half, k, side]
                row_t[half, k, side, :, lane(other)] = src_row[at(df, go), rows(half), lane(other)]
                second[half, k, side] = mover.send(
                    row_t.at[half, k, side], row_b.at[half, k, side], row_to(at(0, go))
                )

    for k, dy in enumerate(order):
        pair[k].wait_recv()
        col_q[k] = src_col[column(dy, 0)] + col_a[k]
        if k == 0:
            ring = {}
            for go, come, side in WAYS:
                ring[side] = mover.send(
                    col_q.at[0, rows(side), :], col_b.at[side], col_to(column(go, 0))
                )

    def join(half, k, df):
        at = slots[half]
        for side in (0, 1):
            second[half, k, side].wait_recv()
        row_q[half, k] = (
            src_row[at(df, 0), rows(half), :] + row_b[half, k, 0] + row_b[half, k, 1]
        )

    for half in (0, 1):
        join(half, 0, 2)
        at = slots[half]
        for go, come, side in WAYS:
            third[half, side] = mover.send(
                row_q.at[half, 0, :, lane(side)], row_c.at[half, side], row_to(at(go, 0))
            )
    yield
    further = {}
    for go, come, side in WAYS:
        k = order.index(go)
        ring[side].wait_recv()
        other = 1 - side
        col_t[side, rows(side), :] = col_q[k, rows(side), :] + col_b[side]
        col_t[side, rows(other), :] = col_q[k, rows(other), :]
        further[side] = mover.send(col_t.at[side], col_c.at[side], col_to(column(go, 0)))
    for k, df in ((1, 1), (2, 3)):
        for half in (0, 1):
            join(half, k, df)
    for half in (0, 1):
        at = slots[half]
        for go, come, side in WAYS:
            k, other = order.index(go), 1 - side
            third[half, side].wait_recv()
            row_u[half, side, :, lane(side)] = row_q[half, k, :, lane(side)] + row_c[half, side]
            row_u[half, side, :, lane(other)] = row_q[half, k, :, lane(other)]
            fourth[half, side] = mover.send(
                row_u.at[half, side], row_d.at[half, side], row_to(at(go, 0))
            )
    yield
    for half in (0, 1):
        join(half, 3, 0)
    for side in (0, 1):
        further[side].wait_recv()
    total = col_q[3] + col_c[0] + col_c[1]
    for half in (0, 1):
        for side in (0, 1):
            fourth[half, side].wait_recv()
        out[rows(half), :] = (
            total[half * HALF:(half + 1) * HALF] + row_q[half, 3] + row_d[half, 0] + row_d[half, 1]
        )
    mover.drain()


def finish(copies):
    for copy in copies:
        copy.wait()


def lanes(x):
    total = x[:, 0:128]
    for k in range(1, x.shape[1] // 128):
        total = total + x[:, k * 128:(k + 1) * 128]
    return total


def reduce_row(mine, land, sems, base):
    r, c, nr, nc = position()
    copies = []
    for o in range(1, nc):
        copies.append(remote(mine, land.at[o - 1], sems, base + o - 1, (r, lax.rem(c + o, nc))))
    for copy in copies:
        copy.start()
    return copies


def reduce_col(mine, land, sems, base):
    r, c, nr, nc = position()
    copies = []
    for o in range(1, nr):
        copies.append(remote(mine, land.at[o - 1], sems, base + o - 1, (lax.rem(r + o, nr), c)))
    for copy in copies:
        copy.start()
    return copies


def total_of(mine, land, n):
    total = mine[...]
    for o in range(n):
        total = total + land[o]
    return total


def tiles_kernel(lists, pts, v, khi, klo, vr, vc, own, pr, pc, psem, vsem):
    r, c, nr, nc = position()
    held = own.shape[0]
    for b in range(held):
        block = 2.0 * pts[:, b * BLK:(b + 1) * BLK]
        own[b] = block
        pr[c * held + b] = block
        pc[r * held + b] = block
    vr[c] = v[...]
    vc[r] = v[...]
    barrier()
    early = []
    for o in range(1, nc):
        to = pr.at[pl.ds(c * held, held)]
        early.append(remote(own, to, psem, len(early), (r, lax.rem(c + o, nc))))
    for o in range(1, nr):
        to = pc.at[pl.ds(r * held, held)]
        early.append(remote(own, to, psem, len(early), (lax.rem(r + o, nr), c)))
    for copy in early:
        copy.start()
    late = spread(v, vr, vc, vsem)
    next(late)
    finish(early)

    def tile(s, _):
        left = pr[lists[0, s]]
        right = pc[lists[1, s]]
        down = jnp.transpose(left)
        for k in range(0, BLK, 32):
            square = None
            for x in range(3):
                offset = down[k:k + 32, x:x + 1] - right[x:x + 1, :]
                square = offset * offset if square is None else square + offset * offset
            scaled = square * lax.rsqrt(jnp.maximum(square, 1e-30))
            remain = jnp.maximum(1.0 - scaled, 0.0)
            remain = remain * remain
            value = remain * remain * (4.0 * scaled + 1.0)
            high = value.astype(BF16)
            khi[s, k:k + 32, :] = high
            klo[s, k:k + 32, :] = (value - high.astype(F32)).astype(BF16)
        return 0

    slots, pauses = lists.shape[1], 7
    for k in range(pauses):
        lax.fori_loop(slots * k // pauses, slots * (k + 1) // pauses, tile, 0)
        next(late, None)


def split(x):
    high = x.astype(BF16)
    low = (x - high.astype(F32)).astype(BF16)
    return high, low


def contract(x, khi, klo, dims):
    n = x.shape[0]
    high, low = split(x)
    both = jnp.concatenate([high, low], axis=0)
    first = lax.dot_general(both, khi, (dims, ((), ())), preferred_element_type=F32)
    second = lax.dot_general(high, klo, (dims, ((), ())), preferred_element_type=F32)
    return first[:n] + first[n:] + second


def apply_kernel(lists, khi, klo, vr, vc, sr, sc):
    r, c, nr, nc = position()
    sr[...] = jnp.zeros_like(sr)
    sc[...] = jnp.zeros_like(sc)
    slots = lists.shape[1]
    live = lax.fori_loop(0, slots, lambda s, n: n + lists[2, s], 0)

    together = 4 if slots % 4 == 0 else 1

    def visit(g, _):
        updates = []
        for k in range(together):
            s = g * together + k
            i, j = lists[0, s], lists[1, s]
            di, dj = lax.shift_right_logical(i, 3), lax.shift_right_logical(j, 3)
            bi = pl.ds(pl.multiple_of((i & 7) * BLK, BLK), BLK)
            bj = pl.ds(pl.multiple_of((j & 7) * BLK, BLK), BLK)
            same = jnp.logical_and(jnp.logical_and(di == c, dj == r), (i & 7) == (j & 7))
            weight = lists[2, s].astype(F32)
            mirror = jnp.where(same, 0.0, weight).astype(F32)
            high, low = khi[s], klo[s]
            ahead = weight * contract(vc[dj, :, bj], high, low, ((1,), (1,)))
            behind = mirror * contract(vr[di, :, bi], high, low, ((1,), (0,)))
            updates.append((di, bi, ahead, dj, bj, behind))
        for di, bi, ahead, dj, bj, behind in updates:
            sr[di, :, bi] += ahead
            sc[dj, :, bj] += behind
        return 0

    lax.fori_loop(0, lax.div(live + together - 1, together), visit, 0)


def merge_kernel(d, sr, sc, w, vr, vc, dots, sums, *rest):
    land, hold = rest[:7], rest[7:12]
    mine, land_a, land_b, csem, vsem, dsem = rest[12:]
    r, c, nr, nc = position()
    barrier()
    for _ in collect(sr, sc, sums, land, hold, csem):
        pass
    image = d[...] + sums[...]
    w[...] = image
    vr[c] = image
    vc[r] = image
    mine[0, 0] = lanes(d[...] * d[...])
    mine[0, 1] = lanes(d[...] * image)
    late = spread(w, vr, vc, vsem)
    next(late)
    first = reduce_row(mine.at[0], land_a, dsem, 0)
    for _ in range(3):
        next(late)
    finish(first)
    mine[1] = total_of(mine.at[0], land_a, nc - 1)
    second = reduce_col(mine.at[1], land_b, dsem, nc - 1)
    for _ in late:
        pass
    finish(second)
    dots[...] = total_of(mine.at[1], land_b, nr - 1)


def local_dots(sr, sc, vr, vc, wr, wc, step):
    fields = sr.shape[1]
    size = 256

    def over(part, dirs, images, n, carry):
        pieces = part.shape[2] // size

        def body(k, carry):
            with_residual, with_direction = carry
            for p in range(pieces):
                cut = slice(p * size, (p + 1) * size)
                direction, image = dirs[k, :, cut], images[k, :, cut]
                product = part[k, :, cut]
                with_residual = with_residual + lanes(product * (direction - step * image))
                with_direction = with_direction + lanes(product * direction)
            return with_residual, with_direction

        return lax.fori_loop(0, n, body, carry)

    zero = jnp.zeros((fields, 128), F32)
    carry = over(sr, vr, wr, sr.shape[0], (zero, zero))
    return over(sc, vc, wc, sc.shape[0], carry)


def final_kernel(d, w, sr, sc, dots, vr, vc, wr, wc, x, res, sums, *rest):
    land, hold = rest[:7], rest[7:12]
    mine, land_a, land_b, csem, dsem = rest[12:]
    r, c, nr, nc = position()
    norm = jnp.sum(dots[0], axis=1, keepdims=True)
    cross = jnp.sum(dots[1], axis=1, keepdims=True)
    step = norm / cross
    residual = d[...] - step * w[...]
    barrier()
    parts = collect(sr, sc, sums, land, hold, csem)
    next(parts)
    with_residual, with_direction = local_dots(sr, sc, vr, vc, wr, wc, step)
    along = lanes(residual * w[...])
    mine[0, 0] = lanes(residual * residual)
    mine[0, 1] = along - step * (along + with_residual)
    mine[0, 2] = along - step * with_direction
    first = reduce_row(mine.at[0], land_a, dsem, 0)
    next(parts)
    finish(first)
    mine[1] = total_of(mine.at[0], land_a, nc - 1)
    second = reduce_col(mine.at[1], land_b, dsem, nc - 1)
    for _ in parts:
        pass
    finish(second)
    totals = total_of(mine.at[1], land_b, nr - 1)
    fresh = jnp.sum(totals[0], axis=1, keepdims=True)
    growth = fresh / norm
    square = jnp.sum(totals[1], axis=1, keepdims=True)
    mixed = jnp.sum(totals[2], axis=1, keepdims=True) + (cross - step * cross)
    stride = fresh / (square + growth * mixed + growth * growth * cross)
    image = w[...] + sums[...]
    direction = residual + growth * d[...]
    applied = w[...] - step * image + growth * w[...]
    x[...] = step * d[...] + stride * direction
    res[...] = residual - stride * applied


def params(cid=None):
    if cid is None:
        return pltpu.CompilerParams(vmem_limit_bytes=24000 * 1024)
    return pltpu.CompilerParams(collective_id=cid, has_side_effects=True, vmem_limit_bytes=24000 * 1024)


def shape(*dims, dtype=F32):
    return jax.ShapeDtypeStruct(dims, dtype)


def local(points, values, tile_lists):
    nr, nc = lax.axis_size("row"), lax.axis_size("col")
    fields, owned = values.shape
    slots = tile_lists.shape[1]
    peers = nr + nc - 2
    sem = lambda n: pltpu.SemaphoreType.DMA((2, n))
    rows, cols = shape(nc, fields, owned), shape(nr, fields, owned)
    tile = shape(slots, BLK, BLK, dtype=BF16)
    part = owned // 2
    landing = [
        pltpu.VMEM((fields, owned), F32),
        pltpu.VMEM((2, SIDE, 2, HALF, part), F32),
        pltpu.VMEM((2, SIDE, 2, HALF, owned), F32),
        pltpu.VMEM((2, 2, HALF, part), F32),
        pltpu.VMEM((2, 2, HALF, owned), F32),
        pltpu.VMEM((SIDE, fields, owned), F32),
        pltpu.VMEM((2, HALF, owned), F32),
        pltpu.VMEM((2, fields, owned), F32),
        pltpu.VMEM((2, SIDE, 2, HALF, owned), F32),
        pltpu.VMEM((2, SIDE, HALF, owned), F32),
        pltpu.VMEM((2, 2, HALF, owned), F32),
        pltpu.VMEM((SIDE, fields, owned), F32),
        pltpu.VMEM((2, fields, owned), F32),
    ]
    ways = 48

    khi, klo, vr, vc = pl.pallas_call(
        tiles_kernel,
        out_shape=(tile, tile, rows, cols),
        in_specs=[SM, VM, VM],
        out_specs=[VM] * 4,
        scratch_shapes=[
            pltpu.VMEM((owned // BLK, 3, BLK), F32),
            pltpu.VMEM((nc * owned // BLK, 3, BLK), F32),
            pltpu.VMEM((nr * owned // BLK, 3, BLK), F32),
            sem(peers), sem(ways),
        ],
        compiler_params=params(0),
        name="gather_and_tiles",
    )(tile_lists, points, values)

    apply = pl.pallas_call(
        apply_kernel,
        out_shape=(rows, cols),
        in_specs=[SM, VM, VM, VM, VM],
        out_specs=[VM] * 2,
        compiler_params=params(),
        name="apply_tiles",
    )
    sr, sc = apply(tile_lists, khi, klo, vr, vc)

    w, wr, wc, dots = pl.pallas_call(
        merge_kernel,
        out_shape=(shape(fields, owned), rows, cols, shape(2, fields, 128)),
        in_specs=[VM] * 3,
        out_specs=[VM] * 4,
        scratch_shapes=landing + [
            pltpu.VMEM((2, 2, fields, 128), F32),
            pltpu.VMEM((nc - 1, 2, fields, 128), F32),
            pltpu.VMEM((nr - 1, 2, fields, 128), F32),
            sem(ways), sem(ways), sem(peers),
        ],
        compiler_params=params(1),
        name="reduce_and_gather",
    )(values, sr, sc)

    sr, sc = apply(tile_lists, khi, klo, wr, wc)

    x, res = pl.pallas_call(
        final_kernel,
        out_shape=(shape(fields, owned), shape(fields, owned)),
        in_specs=[VM] * 9,
        out_specs=[VM] * 2,
        scratch_shapes=landing + [
            pltpu.VMEM((2, 3, fields, 128), F32),
            pltpu.VMEM((nc - 1, 3, fields, 128), F32),
            pltpu.VMEM((nr - 1, 3, fields, 128), F32),
            sem(ways), sem(peers),
        ],
        compiler_params=params(2),
        name="reduce_and_finish",
    )(values, w, sr, sc, dots, vr, vc, wr, wc)
    return x, res


def solution(mesh):
    placed = P(None, ("row", "col"))
    return jax.shard_map(
        local, mesh=mesh, in_specs=(placed,) * 3, out_specs=(placed, placed), check_vma=False
    )
```

```python
import jax
import jax.numpy as jnp
from jax import lax
from jax.experimental import pallas as pl
from jax.experimental.pallas import tpu as pltpu
from jax.sharding import PartitionSpec as P

BLK = 256
MESH = pl.DeviceIdType.MESH
F32 = jnp.float32
BF16 = jnp.bfloat16
VM = pl.BlockSpec(memory_space=pltpu.VMEM)
SM = pl.BlockSpec(memory_space=pltpu.SMEM)


def position():
    nr, nc = lax.axis_size("row"), lax.axis_size("col")
    return lax.axis_index("row"), lax.axis_index("col"), nr, nc


def barrier():
    r, c, nr, nc = position()
    sem = pltpu.get_barrier_semaphore()
    for o in range(1, nc):
        pl.semaphore_signal(sem, 1, device_id=(r, lax.rem(c + o, nc)), device_id_type=MESH)
    for o in range(1, nr):
        pl.semaphore_signal(sem, 1, device_id=(lax.rem(r + o, nr), c), device_id_type=MESH)
    pl.semaphore_wait(sem, nr + nc - 2)


def remote(src, dst, sems, k, to):
    return pltpu.make_async_remote_copy(
        src_ref=src, dst_ref=dst, send_sem=sems.at[0, k], recv_sem=sems.at[1, k],
        device_id=to, device_id_type=MESH,
    )


class Mover:
    def __init__(self, sems):
        self.sems, self.copies = sems, []

    def send(self, src, dst, to):
        copy = remote(src, dst, self.sems, len(self.copies), to)
        copy.start()
        self.copies.append(copy)
        return copy

    def drain(self):
        for copy in self.copies:
            copy.wait_send()


def plane(half):
    r, c, nr, nc = position()
    z, x = lax.div(c, SIDE), lax.rem(c, SIDE)
    first, second = (z, x) if half == 0 else (x, z)

    def slot(df, dg):
        f, g = lax.rem(first + df, SIDE), lax.rem(second + dg, SIDE)
        return f * SIDE + g if half == 0 else g * SIDE + f

    return slot


def column(dy, dcore):
    r, c, nr, nc = position()
    y, core = lax.div(r, 2), lax.rem(r, 2)
    return lax.rem(y + dy, SIDE) * 2 + lax.rem(core + dcore, 2)


HALF = 8
SIDE = 4
WAYS = ((1, 3, 0), (3, 1, 1))


def spread(src, by_row, by_col, sems):
    r, c, nr, nc = position()
    mover = Mover(sems)
    owned = src.shape[1]
    part = owned // 2
    row_to = lambda slot: (r, slot)
    col_to = lambda slot: (slot, c)

    def cell(half, slot, side=None):
        rows = pl.ds(half * HALF, HALF)
        if side is None:
            return by_row.at[slot, rows, :]
        return by_row.at[slot, rows, pl.ds(side * part, part)]

    slots = [plane(0), plane(1)]
    near, far, cross, away = {}, {}, {}, {}
    own = [src.at[pl.ds(half * HALF, HALF), :] for half in (0, 1)]
    for half in (0, 1):
        at = slots[half]
        for go, come, side in WAYS:
            near[half, side] = mover.send(own[half], cell(half, at(0, 0)), row_to(at(go, 0)))
    ring, pair = {}, []
    for go, come, side in WAYS:
        ring[side] = mover.send(src, by_col.at[r], col_to(column(go, 0)))
    pair.append(mover.send(src, by_col.at[r], col_to(column(0, 1))))
    for half in (0, 1):
        at = slots[half]
        for go, come, side in WAYS:
            cross[half, 0, side] = mover.send(own[half], cell(half, at(0, 0)), row_to(at(0, go)))
    yield
    for half in (0, 1):
        at = slots[half]
        for go, come, side in WAYS:
            near[half, side].wait_recv()
            from_slot = at(come, 0)
            far[half, side] = mover.send(
                cell(half, from_slot, side), cell(half, from_slot, side), row_to(at(go, 0))
            )
    for half in (0, 1):
        at = slots[half]
        for _, come, _ in WAYS:
            from_slot = at(come, 0)
            for go, _, side in WAYS:
                cross[half, come, side] = mover.send(
                    cell(half, from_slot), cell(half, from_slot), row_to(at(0, go))
                )
    yield
    further = {}
    for go, come, side in WAYS:
        ring[side].wait_recv()
        rows = pl.ds(side * HALF, HALF)
        from_slot = column(come, 0)
        further[side] = mover.send(
            by_col.at[from_slot, rows, :], by_col.at[from_slot, rows, :], col_to(column(go, 0))
        )
    for _, come, _ in WAYS:
        from_slot = column(come, 0)
        pair.append(mover.send(by_col.at[from_slot], by_col.at[from_slot], col_to(column(0, 1))))

    def pass_on(half, df):
        at = slots[half]
        for go, come, side in WAYS:
            cross[half, df, side].wait_recv()
            from_slot = at(df, come)
            away[half, df, side] = mover.send(
                cell(half, from_slot, side), cell(half, from_slot, side), row_to(at(0, go))
            )

    for half in (0, 1):
        pass_on(half, 0)
    yield
    for half in (0, 1):
        at = slots[half]
        for side in (0, 1):
            far[half, side].wait_recv()
        from_slot = at(2, 0)
        for go, _, side in WAYS:
            cross[half, 2, side] = mover.send(
                cell(half, from_slot), cell(half, from_slot), row_to(at(0, go))
            )
    for side in (0, 1):
        further[side].wait_recv()
    from_slot = column(2, 0)
    pair.append(mover.send(by_col.at[from_slot], by_col.at[from_slot], col_to(column(0, 1))))
    yield
    for df in (3, 1):
        for half in (0, 1):
            pass_on(half, df)
        yield
    for half in (0, 1):
        pass_on(half, 2)
    yield
    for df in (0, 3, 1, 2):
        for half in (0, 1):
            for side in (0, 1):
                away[half, df, side].wait_recv()
    for copy in pair:
        copy.wait_recv()
    mover.drain()


def collect(src_row, src_col, out, land, hold, sems):
    r, c, nr, nc = position()
    mover = Mover(sems)
    row_a, row_b, row_c, row_d, col_a, col_b, col_c = land
    row_t, row_q, row_u, col_q, col_t = hold
    owned = out.shape[1]
    part = owned // 2
    row_to = lambda slot: (r, slot)
    col_to = lambda slot: (slot, c)
    slots = [plane(0), plane(1)]
    lane = lambda side: pl.ds(side * part, part)
    rows = lambda half: pl.ds(half * HALF, HALF)
    first, second, third, fourth = {}, {}, {}, {}
    order = (2, 1, 3, 0)

    pair = []
    for k, dy in enumerate(order):
        pair.append(mover.send(src_col.at[column(dy, 1)], col_a.at[k], col_to(column(0, 1))))
    for k, df in enumerate(order):
        for half in (0, 1):
            at = slots[half]
            for go, come, side in WAYS:
                first[half, k, side] = mover.send(
                    src_row.at[at(df, 2), rows(half), lane(side)], row_a.at[half, k, side],
                    row_to(at(0, go)),
                )
    yield
    for k, df in enumerate(order):
        for half in (0, 1):
            at = slots[half]
            for go, come, side in WAYS:
                first[half, k, side].wait_recv()
                keep, other = src_row[at(df, go), rows(half), lane(side)], 1 - side
                row_t[half, k, side, :, lane(side)] = keep + row_a[half, k, side]
                row_t[half, k, side, :, lane(other)] = src_row[at(df, go), rows(half), lane(other)]
                second[half, k, side] = mover.send(
                    row_t.at[half, k, side], row_b.at[half, k, side], row_to(at(0, go))
                )

    for k, dy in enumerate(order):
        pair[k].wait_recv()
        col_q[k] = src_col[column(dy, 0)] + col_a[k]
        if k == 0:
            ring = {}
            for go, come, side in WAYS:
                ring[side] = mover.send(
                    col_q.at[0, rows(side), :], col_b.at[side], col_to(column(go, 0))
                )

    def join(half, k, df):
        at = slots[half]
        for side in (0, 1):
            second[half, k, side].wait_recv()
        row_q[half, k] = (
            src_row[at(df, 0), rows(half), :] + row_b[half, k, 0] + row_b[half, k, 1]
        )

    for half in (0, 1):
        join(half, 0, 2)
        at = slots[half]
        for go, come, side in WAYS:
            third[half, side] = mover.send(
                row_q.at[half, 0, :, lane(side)], row_c.at[half, side], row_to(at(go, 0))
            )
    yield
    further = {}
    for go, come, side in WAYS:
        k = order.index(go)
        ring[side].wait_recv()
        other = 1 - side
        col_t[side, rows(side), :] = col_q[k, rows(side), :] + col_b[side]
        col_t[side, rows(other), :] = col_q[k, rows(other), :]
        further[side] = mover.send(col_t.at[side], col_c.at[side], col_to(column(go, 0)))
    for k, df in ((1, 1), (2, 3)):
        for half in (0, 1):
            join(half, k, df)
    for half in (0, 1):
        at = slots[half]
        for go, come, side in WAYS:
            k, other = order.index(go), 1 - side
            third[half, side].wait_recv()
            row_u[half, side, :, lane(side)] = row_q[half, k, :, lane(side)] + row_c[half, side]
            row_u[half, side, :, lane(other)] = row_q[half, k, :, lane(other)]
            fourth[half, side] = mover.send(
                row_u.at[half, side], row_d.at[half, side], row_to(at(go, 0))
            )
    yield
    for half in (0, 1):
        join(half, 3, 0)
    for side in (0, 1):
        further[side].wait_recv()
    total = col_q[3] + col_c[0] + col_c[1]
    for half in (0, 1):
        for side in (0, 1):
            fourth[half, side].wait_recv()
        out[rows(half), :] = (
            total[half * HALF:(half + 1) * HALF] + row_q[half, 3] + row_d[half, 0] + row_d[half, 1]
        )
    mover.drain()


def finish(copies):
    for copy in copies:
        copy.wait()


def lanes(x):
    total = x[:, 0:128]
    for k in range(1, x.shape[1] // 128):
        total = total + x[:, k * 128:(k + 1) * 128]
    return total


def reduce_row(mine, land, sems, base):
    r, c, nr, nc = position()
    copies = []
    for o in range(1, nc):
        copies.append(remote(mine, land.at[o - 1], sems, base + o - 1, (r, lax.rem(c + o, nc))))
    for copy in copies:
        copy.start()
    return copies


def reduce_col(mine, land, sems, base):
    r, c, nr, nc = position()
    copies = []
    for o in range(1, nr):
        copies.append(remote(mine, land.at[o - 1], sems, base + o - 1, (lax.rem(r + o, nr), c)))
    for copy in copies:
        copy.start()
    return copies


def total_of(mine, land, n):
    total = mine[...]
    for o in range(n):
        total = total + land[o]
    return total


def tiles_kernel(lists, pts, v, khi, klo, vr, vc, own, pr, pc, psem, vsem):
    r, c, nr, nc = position()
    held = own.shape[0]
    for b in range(held):
        block = 2.0 * pts[:, b * BLK:(b + 1) * BLK]
        own[b] = block
        pr[c * held + b] = block
        pc[r * held + b] = block
    vr[c] = v[...]
    vc[r] = v[...]
    barrier()
    early = []
    for o in range(1, nc):
        to = pr.at[pl.ds(c * held, held)]
        early.append(remote(own, to, psem, len(early), (r, lax.rem(c + o, nc))))
    for o in range(1, nr):
        to = pc.at[pl.ds(r * held, held)]
        early.append(remote(own, to, psem, len(early), (lax.rem(r + o, nr), c)))
    for copy in early:
        copy.start()
    late = spread(v, vr, vc, vsem)
    next(late)
    finish(early)

    def tile(s, _):
        left = pr[lists[0, s]]
        right = pc[lists[1, s]]
        down = jnp.transpose(left)
        for k in range(0, BLK, 32):
            square = None
            for x in range(3):
                offset = down[k:k + 32, x:x + 1] - right[x:x + 1, :]
                square = offset * offset if square is None else square + offset * offset
            scaled = square * lax.rsqrt(jnp.maximum(square, 1e-30))
            remain = jnp.maximum(1.0 - scaled, 0.0)
            remain = remain * remain
            value = remain * remain * (4.0 * scaled + 1.0)
            high = value.astype(BF16)
            khi[s, k:k + 32, :] = high
            klo[s, k:k + 32, :] = (value - high.astype(F32)).astype(BF16)
        return 0

    slots, pauses = lists.shape[1], 7
    for k in range(pauses):
        lax.fori_loop(slots * k // pauses, slots * (k + 1) // pauses, tile, 0)
        next(late, None)


def split(x):
    high = x.astype(BF16)
    low = (x - high.astype(F32)).astype(BF16)
    return high, low


def contract(x, khi, klo, dims):
    n = x.shape[0]
    high, low = split(x)
    both = jnp.concatenate([high, low], axis=0)
    first = lax.dot_general(both, khi, (dims, ((), ())), preferred_element_type=F32)
    second = lax.dot_general(high, klo, (dims, ((), ())), preferred_element_type=F32)
    return first[:n] + first[n:] + second


def apply_kernel(lists, khi, klo, vr, vc, sr, sc):
    r, c, nr, nc = position()
    sr[...] = jnp.zeros_like(sr)
    sc[...] = jnp.zeros_like(sc)
    slots = lists.shape[1]
    live = lax.fori_loop(0, slots, lambda s, n: n + lists[2, s], 0)

    together = 4 if slots % 4 == 0 else 1

    def visit(g, _):
        updates = []
        for k in range(together):
            s = g * together + k
            i, j = lists[0, s], lists[1, s]
            di, dj = lax.shift_right_logical(i, 3), lax.shift_right_logical(j, 3)
            bi = pl.ds(pl.multiple_of((i & 7) * BLK, BLK), BLK)
            bj = pl.ds(pl.multiple_of((j & 7) * BLK, BLK), BLK)
            same = jnp.logical_and(jnp.logical_and(di == c, dj == r), (i & 7) == (j & 7))
            weight = lists[2, s].astype(F32)
            mirror = jnp.where(same, 0.0, weight).astype(F32)
            high, low = khi[s], klo[s]
            ahead = weight * contract(vc[dj, :, bj], high, low, ((1,), (1,)))
            behind = mirror * contract(vr[di, :, bi], high, low, ((1,), (0,)))
            updates.append((di, bi, ahead, dj, bj, behind))
        for di, bi, ahead, dj, bj, behind in updates:
            sr[di, :, bi] += ahead
            sc[dj, :, bj] += behind
        return 0

    lax.fori_loop(0, lax.div(live + together - 1, together), visit, 0)


def local_dot(sr, sc, dr, dc):
    fields = sr.shape[1]

    def over(part, vectors, carry):
        body = lambda k, total: total + lanes(part[k] * vectors[k])
        return lax.fori_loop(0, part.shape[0], body, carry)

    return over(sc, dc, over(sr, dr, jnp.zeros((fields, 128), F32)))


def merge_kernel(d, sr, sc, dr, dc, w, vr, vc, dots, sums, *rest):
    land, hold = rest[:7], rest[7:12]
    mine, land_a, land_b, csem, vsem, dsem = rest[12:]
    r, c, nr, nc = position()
    barrier()
    parts = collect(sr, sc, sums, land, hold, csem)
    next(parts)
    square = lanes(d[...] * d[...])
    mine[0, 0] = square
    mine[0, 1] = square + local_dot(sr, sc, dr, dc)
    first = reduce_row(mine.at[0], land_a, dsem, 0)
    next(parts)
    finish(first)
    mine[1] = total_of(mine.at[0], land_a, nc - 1)
    second = reduce_col(mine.at[1], land_b, dsem, nc - 1)
    for _ in parts:
        pass
    image = d[...] + sums[...]
    w[...] = image
    vr[c] = image
    vc[r] = image
    late = spread(w, vr, vc, vsem)
    next(late)
    finish(second)
    dots[...] = total_of(mine.at[1], land_b, nr - 1)
    for _ in late:
        pass


def local_dots(sr, sc, vr, vc, wr, wc, step):
    fields = sr.shape[1]
    size = 256

    def over(part, dirs, images, n, carry):
        pieces = part.shape[2] // size

        def body(k, carry):
            with_residual, with_direction = carry
            for p in range(pieces):
                cut = slice(p * size, (p + 1) * size)
                direction, image = dirs[k, :, cut], images[k, :, cut]
                product = part[k, :, cut]
                with_residual = with_residual + lanes(product * (direction - step * image))
                with_direction = with_direction + lanes(product * direction)
            return with_residual, with_direction

        return lax.fori_loop(0, n, body, carry)

    zero = jnp.zeros((fields, 128), F32)
    carry = over(sr, vr, wr, sr.shape[0], (zero, zero))
    return over(sc, vc, wc, sc.shape[0], carry)


def final_kernel(d, w, sr, sc, dots, vr, vc, wr, wc, x, res, sums, *rest):
    land, hold = rest[:7], rest[7:12]
    mine, land_a, land_b, csem, dsem = rest[12:]
    r, c, nr, nc = position()
    norm = jnp.sum(dots[0], axis=1, keepdims=True)
    cross = jnp.sum(dots[1], axis=1, keepdims=True)
    step = norm / cross
    residual = d[...] - step * w[...]
    barrier()
    parts = collect(sr, sc, sums, land, hold, csem)
    next(parts)
    with_residual, with_direction = local_dots(sr, sc, vr, vc, wr, wc, step)
    along = lanes(residual * w[...])
    mine[0, 0] = lanes(residual * residual)
    mine[0, 1] = along - step * (along + with_residual)
    mine[0, 2] = along - step * with_direction
    first = reduce_row(mine.at[0], land_a, dsem, 0)
    next(parts)
    finish(first)
    mine[1] = total_of(mine.at[0], land_a, nc - 1)
    second = reduce_col(mine.at[1], land_b, dsem, nc - 1)
    for _ in parts:
        pass
    finish(second)
    totals = total_of(mine.at[1], land_b, nr - 1)
    fresh = jnp.sum(totals[0], axis=1, keepdims=True)
    growth = fresh / norm
    square = jnp.sum(totals[1], axis=1, keepdims=True)
    mixed = jnp.sum(totals[2], axis=1, keepdims=True) + (cross - step * cross)
    stride = fresh / (square + growth * mixed + growth * growth * cross)
    image = w[...] + sums[...]
    direction = residual + growth * d[...]
    applied = w[...] - step * image + growth * w[...]
    x[...] = step * d[...] + stride * direction
    res[...] = residual - stride * applied


def params(cid=None):
    if cid is None:
        return pltpu.CompilerParams(vmem_limit_bytes=24000 * 1024)
    return pltpu.CompilerParams(collective_id=cid, has_side_effects=True, vmem_limit_bytes=24000 * 1024)


def shape(*dims, dtype=F32):
    return jax.ShapeDtypeStruct(dims, dtype)


def local(points, values, tile_lists):
    nr, nc = lax.axis_size("row"), lax.axis_size("col")
    fields, owned = values.shape
    slots = tile_lists.shape[1]
    peers = nr + nc - 2
    sem = lambda n: pltpu.SemaphoreType.DMA((2, n))
    rows, cols = shape(nc, fields, owned), shape(nr, fields, owned)
    tile = shape(slots, BLK, BLK, dtype=BF16)
    part = owned // 2
    landing = [
        pltpu.VMEM((fields, owned), F32),
        pltpu.VMEM((2, SIDE, 2, HALF, part), F32),
        pltpu.VMEM((2, SIDE, 2, HALF, owned), F32),
        pltpu.VMEM((2, 2, HALF, part), F32),
        pltpu.VMEM((2, 2, HALF, owned), F32),
        pltpu.VMEM((SIDE, fields, owned), F32),
        pltpu.VMEM((2, HALF, owned), F32),
        pltpu.VMEM((2, fields, owned), F32),
        pltpu.VMEM((2, SIDE, 2, HALF, owned), F32),
        pltpu.VMEM((2, SIDE, HALF, owned), F32),
        pltpu.VMEM((2, 2, HALF, owned), F32),
        pltpu.VMEM((SIDE, fields, owned), F32),
        pltpu.VMEM((2, fields, owned), F32),
    ]
    ways = 48

    khi, klo, vr, vc = pl.pallas_call(
        tiles_kernel,
        out_shape=(tile, tile, rows, cols),
        in_specs=[SM, VM, VM],
        out_specs=[VM] * 4,
        scratch_shapes=[
            pltpu.VMEM((owned // BLK, 3, BLK), F32),
            pltpu.VMEM((nc * owned // BLK, 3, BLK), F32),
            pltpu.VMEM((nr * owned // BLK, 3, BLK), F32),
            sem(peers), sem(ways),
        ],
        compiler_params=params(0),
        name="gather_and_tiles",
    )(tile_lists, points, values)

    apply = pl.pallas_call(
        apply_kernel,
        out_shape=(rows, cols),
        in_specs=[SM, VM, VM, VM, VM],
        out_specs=[VM] * 2,
        compiler_params=params(),
        name="apply_tiles",
    )
    sr, sc = apply(tile_lists, khi, klo, vr, vc)

    w, wr, wc, dots = pl.pallas_call(
        merge_kernel,
        out_shape=(shape(fields, owned), rows, cols, shape(2, fields, 128)),
        in_specs=[VM] * 5,
        out_specs=[VM] * 4,
        scratch_shapes=landing + [
            pltpu.VMEM((2, 2, fields, 128), F32),
            pltpu.VMEM((nc - 1, 2, fields, 128), F32),
            pltpu.VMEM((nr - 1, 2, fields, 128), F32),
            sem(ways), sem(ways), sem(peers),
        ],
        compiler_params=params(1),
        name="reduce_and_gather",
    )(values, sr, sc, vr, vc)

    sr, sc = apply(tile_lists, khi, klo, wr, wc)

    x, res = pl.pallas_call(
        final_kernel,
        out_shape=(shape(fields, owned), shape(fields, owned)),
        in_specs=[VM] * 9,
        out_specs=[VM] * 2,
        scratch_shapes=landing + [
            pltpu.VMEM((2, 3, fields, 128), F32),
            pltpu.VMEM((nc - 1, 3, fields, 128), F32),
            pltpu.VMEM((nr - 1, 3, fields, 128), F32),
            sem(ways), sem(peers),
        ],
        compiler_params=params(2),
        name="reduce_and_finish",
    )(values, w, sr, sc, dots, vr, vc, wr, wc)
    return x, res


def solution(mesh):
    placed = P(None, ("row", "col"))
    return jax.shard_map(
        local, mesh=mesh, in_specs=(placed,) * 3, out_specs=(placed, placed), check_vma=False
    )
```

```python
import jax
import jax.numpy as jnp
from jax import lax
from jax.experimental import pallas as pl
from jax.experimental.pallas import tpu as pltpu
from jax.sharding import PartitionSpec as P

BLK = 256
MESH = pl.DeviceIdType.MESH
F32 = jnp.float32
BF16 = jnp.bfloat16
VM = pl.BlockSpec(memory_space=pltpu.VMEM)
SM = pl.BlockSpec(memory_space=pltpu.SMEM)


def position():
    nr, nc = lax.axis_size("row"), lax.axis_size("col")
    return lax.axis_index("row"), lax.axis_index("col"), nr, nc


def barrier():
    r, c, nr, nc = position()
    sem = pltpu.get_barrier_semaphore()
    for o in range(1, nc):
        pl.semaphore_signal(sem, 1, device_id=(r, lax.rem(c + o, nc)), device_id_type=MESH)
    for o in range(1, nr):
        pl.semaphore_signal(sem, 1, device_id=(lax.rem(r + o, nr), c), device_id_type=MESH)
    pl.semaphore_wait(sem, nr + nc - 2)


def remote(src, dst, sems, k, to):
    return pltpu.make_async_remote_copy(
        src_ref=src, dst_ref=dst, send_sem=sems.at[0, k], recv_sem=sems.at[1, k],
        device_id=to, device_id_type=MESH,
    )


class Mover:
    def __init__(self, sems):
        self.sems, self.copies = sems, []

    def send(self, src, dst, to):
        copy = remote(src, dst, self.sems, len(self.copies), to)
        copy.start()
        self.copies.append(copy)
        return copy

    def drain(self):
        for copy in self.copies:
            copy.wait_send()


def plane(half):
    r, c, nr, nc = position()
    z, x = lax.div(c, SIDE), lax.rem(c, SIDE)
    first, second = (z, x) if half == 0 else (x, z)

    def slot(df, dg):
        f, g = lax.rem(first + df, SIDE), lax.rem(second + dg, SIDE)
        return f * SIDE + g if half == 0 else g * SIDE + f

    return slot


def column(dy, dcore):
    r, c, nr, nc = position()
    y, core = lax.div(r, 2), lax.rem(r, 2)
    return lax.rem(y + dy, SIDE) * 2 + lax.rem(core + dcore, 2)


HALF = 8
SIDE = 4
WAYS = ((1, 3, 0), (3, 1, 1))


def spread(src, by_row, by_col, sems):
    r, c, nr, nc = position()
    mover = Mover(sems)
    owned = src.shape[1]
    part = owned // 2
    row_to = lambda slot: (r, slot)
    col_to = lambda slot: (slot, c)

    def cell(half, slot, side=None):
        rows = pl.ds(half * HALF, HALF)
        if side is None:
            return by_row.at[slot, rows, :]
        return by_row.at[slot, rows, pl.ds(side * part, part)]

    slots = [plane(0), plane(1)]
    near, far, cross, away = {}, {}, {}, {}
    own = [src.at[pl.ds(half * HALF, HALF), :] for half in (0, 1)]
    for half in (0, 1):
        at = slots[half]
        for go, come, side in WAYS:
            near[half, side] = mover.send(own[half], cell(half, at(0, 0)), row_to(at(go, 0)))
    ring, pair = {}, []
    for go, come, side in WAYS:
        ring[side] = mover.send(src, by_col.at[r], col_to(column(go, 0)))
    pair.append(mover.send(src, by_col.at[r], col_to(column(0, 1))))
    for half in (0, 1):
        at = slots[half]
        for go, come, side in WAYS:
            cross[half, 0, side] = mover.send(own[half], cell(half, at(0, 0)), row_to(at(0, go)))
    yield
    for half in (0, 1):
        at = slots[half]
        for go, come, side in WAYS:
            near[half, side].wait_recv()
            from_slot = at(come, 0)
            far[half, side] = mover.send(
                cell(half, from_slot, side), cell(half, from_slot, side), row_to(at(go, 0))
            )
    for half in (0, 1):
        at = slots[half]
        for _, come, _ in WAYS:
            from_slot = at(come, 0)
            for go, _, side in WAYS:
                cross[half, come, side] = mover.send(
                    cell(half, from_slot), cell(half, from_slot), row_to(at(0, go))
                )
    yield
    further = {}
    for go, come, side in WAYS:
        ring[side].wait_recv()
        rows = pl.ds(side * HALF, HALF)
        from_slot = column(come, 0)
        further[side] = mover.send(
            by_col.at[from_slot, rows, :], by_col.at[from_slot, rows, :], col_to(column(go, 0))
        )
    for _, come, _ in WAYS:
        from_slot = column(come, 0)
        pair.append(mover.send(by_col.at[from_slot], by_col.at[from_slot], col_to(column(0, 1))))

    def pass_on(half, df):
        at = slots[half]
        for go, come, side in WAYS:
            cross[half, df, side].wait_recv()
            from_slot = at(df, come)
            away[half, df, side] = mover.send(
                cell(half, from_slot, side), cell(half, from_slot, side), row_to(at(0, go))
            )

    for half in (0, 1):
        pass_on(half, 0)
    yield
    for half in (0, 1):
        at = slots[half]
        for side in (0, 1):
            far[half, side].wait_recv()
        from_slot = at(2, 0)
        for go, _, side in WAYS:
            cross[half, 2, side] = mover.send(
                cell(half, from_slot), cell(half, from_slot), row_to(at(0, go))
            )
    for side in (0, 1):
        further[side].wait_recv()
    from_slot = column(2, 0)
    pair.append(mover.send(by_col.at[from_slot], by_col.at[from_slot], col_to(column(0, 1))))
    yield
    for df in (3, 1):
        for half in (0, 1):
            pass_on(half, df)
        yield
    for half in (0, 1):
        pass_on(half, 2)
    yield
    for df in (0, 3, 1, 2):
        for half in (0, 1):
            for side in (0, 1):
                away[half, df, side].wait_recv()
    for copy in pair:
        copy.wait_recv()
    mover.drain()


def collect(src_row, src_col, out, land, hold, sems):
    r, c, nr, nc = position()
    mover = Mover(sems)
    row_a, row_b, row_c, row_d, col_a, col_b, col_c = land
    row_t, row_q, row_u, col_q, col_t = hold
    owned = out.shape[1]
    part = owned // 2
    row_to = lambda slot: (r, slot)
    col_to = lambda slot: (slot, c)
    slots = [plane(0), plane(1)]
    lane = lambda side: pl.ds(side * part, part)
    rows = lambda half: pl.ds(half * HALF, HALF)
    first, second, third, fourth = {}, {}, {}, {}
    order = (2, 1, 3, 0)

    pair = []
    for k, dy in enumerate(order):
        pair.append(mover.send(src_col.at[column(dy, 1)], col_a.at[k], col_to(column(0, 1))))
    for k, df in enumerate(order):
        for half in (0, 1):
            at = slots[half]
            for go, come, side in WAYS:
                first[half, k, side] = mover.send(
                    src_row.at[at(df, 2), rows(half), lane(side)], row_a.at[half, k, side],
                    row_to(at(0, go)),
                )
    yield
    for k, df in enumerate(order):
        for half in (0, 1):
            at = slots[half]
            for go, come, side in WAYS:
                first[half, k, side].wait_recv()
                keep, other = src_row[at(df, go), rows(half), lane(side)], 1 - side
                row_t[half, k, side, :, lane(side)] = keep + row_a[half, k, side]
                row_t[half, k, side, :, lane(other)] = src_row[at(df, go), rows(half), lane(other)]
                second[half, k, side] = mover.send(
                    row_t.at[half, k, side], row_b.at[half, k, side], row_to(at(0, go))
                )

    for k, dy in enumerate(order):
        pair[k].wait_recv()
        col_q[k] = src_col[column(dy, 0)] + col_a[k]
        if k == 0:
            ring = {}
            for go, come, side in WAYS:
                ring[side] = mover.send(
                    col_q.at[0, rows(side), :], col_b.at[side], col_to(column(go, 0))
                )

    def join(half, k, df):
        at = slots[half]
        for side in (0, 1):
            second[half, k, side].wait_recv()
        row_q[half, k] = (
            src_row[at(df, 0), rows(half), :] + row_b[half, k, 0] + row_b[half, k, 1]
        )

    for half in (0, 1):
        join(half, 0, 2)
        at = slots[half]
        for go, come, side in WAYS:
            third[half, side] = mover.send(
                row_q.at[half, 0, :, lane(side)], row_c.at[half, side], row_to(at(go, 0))
            )
    yield
    further = {}
    for go, come, side in WAYS:
        k = order.index(go)
        ring[side].wait_recv()
        other = 1 - side
        col_t[side, rows(side), :] = col_q[k, rows(side), :] + col_b[side]
        col_t[side, rows(other), :] = col_q[k, rows(other), :]
        further[side] = mover.send(col_t.at[side], col_c.at[side], col_to(column(go, 0)))
    for k, df in ((1, 1), (2, 3)):
        for half in (0, 1):
            join(half, k, df)
    for half in (0, 1):
        at = slots[half]
        for go, come, side in WAYS:
            k, other = order.index(go), 1 - side
            third[half, side].wait_recv()
            row_u[half, side, :, lane(side)] = row_q[half, k, :, lane(side)] + row_c[half, side]
            row_u[half, side, :, lane(other)] = row_q[half, k, :, lane(other)]
            fourth[half, side] = mover.send(
                row_u.at[half, side], row_d.at[half, side], row_to(at(go, 0))
            )
    yield
    for half in (0, 1):
        join(half, 3, 0)
    for side in (0, 1):
        further[side].wait_recv()
    total = col_q[3] + col_c[0] + col_c[1]
    for half in (0, 1):
        for side in (0, 1):
            fourth[half, side].wait_recv()
        out[rows(half), :] = (
            total[half * HALF:(half + 1) * HALF] + row_q[half, 3] + row_d[half, 0] + row_d[half, 1]
        )
    mover.drain()


def finish(copies):
    for copy in copies:
        copy.wait()


def lanes(x):
    total = x[:, 0:128]
    for k in range(1, x.shape[1] // 128):
        total = total + x[:, k * 128:(k + 1) * 128]
    return total


def reduce_row(mine, land, sems, base):
    r, c, nr, nc = position()
    copies = []
    for o in range(1, nc):
        copies.append(remote(mine, land.at[o - 1], sems, base + o - 1, (r, lax.rem(c + o, nc))))
    for copy in copies:
        copy.start()
    return copies


def reduce_col(mine, land, sems, base):
    r, c, nr, nc = position()
    copies = []
    for o in range(1, nr):
        copies.append(remote(mine, land.at[o - 1], sems, base + o - 1, (lax.rem(r + o, nr), c)))
    for copy in copies:
        copy.start()
    return copies


def total_of(mine, land, n):
    total = mine[...]
    for o in range(n):
        total = total + land[o]
    return total


def tiles_kernel(lists, pts, v, khi, klo, vr, vc, own, pr, pc, psem, vsem):
    r, c, nr, nc = position()
    held = own.shape[0]
    for b in range(held):
        block = 2.0 * pts[:, b * BLK:(b + 1) * BLK]
        own[b] = block
        pr[c * held + b] = block
        pc[r * held + b] = block
    vr[c] = v[...]
    vc[r] = v[...]
    barrier()
    early = []
    for o in range(1, nc):
        to = pr.at[pl.ds(c * held, held)]
        early.append(remote(own, to, psem, len(early), (r, lax.rem(c + o, nc))))
    for o in range(1, nr):
        to = pc.at[pl.ds(r * held, held)]
        early.append(remote(own, to, psem, len(early), (lax.rem(r + o, nr), c)))
    for copy in early:
        copy.start()
    late = spread(v, vr, vc, vsem)
    next(late)
    finish(early)

    def tile(s, _):
        left = pr[lists[0, s]]
        right = pc[lists[1, s]]
        down = jnp.transpose(left)
        for k in range(0, BLK, 32):
            square = None
            for x in range(3):
                offset = down[k:k + 32, x:x + 1] - right[x:x + 1, :]
                square = offset * offset if square is None else square + offset * offset
            scaled = square * lax.rsqrt(jnp.maximum(square, 1e-30))
            remain = jnp.maximum(1.0 - scaled, 0.0)
            remain = remain * remain
            value = remain * remain * (4.0 * scaled + 1.0)
            high = value.astype(BF16)
            khi[s, k:k + 32, :] = high
            klo[s, k:k + 32, :] = (value - high.astype(F32)).astype(BF16)
        return 0

    slots, pauses = lists.shape[1], 6
    for k in range(pauses):
        next(late)
        lax.fori_loop(slots * k // pauses, slots * (k + 1) // pauses, tile, 0)
    for _ in late:
        pass


def split(x):
    high = x.astype(BF16)
    low = (x - high.astype(F32)).astype(BF16)
    return high, low


def contract(x, khi, klo, dims):
    n = x.shape[0]
    high, low = split(x)
    both = jnp.concatenate([high, low], axis=0)
    first = lax.dot_general(both, khi, (dims, ((), ())), preferred_element_type=F32)
    second = lax.dot_general(high, klo, (dims, ((), ())), preferred_element_type=F32)
    return first[:n] + first[n:] + second


def apply_kernel(lists, khi, klo, vr, vc, sr, sc):
    r, c, nr, nc = position()
    sr[...] = jnp.zeros_like(sr)
    sc[...] = jnp.zeros_like(sc)
    slots = lists.shape[1]
    live = lax.fori_loop(0, slots, lambda s, n: n + lists[2, s], 0)

    together = 4 if slots % 4 == 0 else 1

    def visit(g, _):
        updates = []
        for k in range(together):
            s = g * together + k
            i, j = lists[0, s], lists[1, s]
            di, dj = lax.shift_right_logical(i, 3), lax.shift_right_logical(j, 3)
            bi = pl.ds(pl.multiple_of((i & 7) * BLK, BLK), BLK)
            bj = pl.ds(pl.multiple_of((j & 7) * BLK, BLK), BLK)
            same = jnp.logical_and(jnp.logical_and(di == c, dj == r), (i & 7) == (j & 7))
            weight = lists[2, s].astype(F32)
            mirror = jnp.where(same, 0.0, weight).astype(F32)
            high, low = khi[s], klo[s]
            ahead = weight * contract(vc[dj, :, bj], high, low, ((1,), (1,)))
            behind = mirror * contract(vr[di, :, bi], high, low, ((1,), (0,)))
            updates.append((di, bi, ahead, dj, bj, behind))
        for di, bi, ahead, dj, bj, behind in updates:
            sr[di, :, bi] += ahead
            sc[dj, :, bj] += behind
        return 0

    lax.fori_loop(0, lax.div(live + together - 1, together), visit, 0)


def local_dot(sr, sc, dr, dc):
    fields = sr.shape[1]

    def over(part, vectors, carry):
        body = lambda k, total: total + lanes(part[k] * vectors[k])
        return lax.fori_loop(0, part.shape[0], body, carry)

    return over(sc, dc, over(sr, dr, jnp.zeros((fields, 128), F32)))


def merge_kernel(d, sr, sc, dr, dc, w, vr, vc, dots, sums, *rest):
    land, hold = rest[:7], rest[7:12]
    mine, land_a, land_b, csem, vsem, dsem = rest[12:]
    r, c, nr, nc = position()
    barrier()
    parts = collect(sr, sc, sums, land, hold, csem)
    next(parts)
    square = lanes(d[...] * d[...])
    mine[0, 0] = square
    mine[0, 1] = square + local_dot(sr, sc, dr, dc)
    first = reduce_row(mine.at[0], land_a, dsem, 0)
    next(parts)
    finish(first)
    mine[1] = total_of(mine.at[0], land_a, nc - 1)
    second = reduce_col(mine.at[1], land_b, dsem, nc - 1)
    for _ in parts:
        pass
    image = d[...] + sums[...]
    w[...] = image
    vr[c] = image
    vc[r] = image
    late = spread(w, vr, vc, vsem)
    next(late)
    finish(second)
    dots[...] = total_of(mine.at[1], land_b, nr - 1)
    for _ in late:
        pass


def local_dots(sr, sc, vr, vc, wr, wc, step):
    fields = sr.shape[1]
    size = 256

    def over(part, dirs, images, n, carry):
        pieces = part.shape[2] // size

        def body(k, carry):
            with_residual, with_direction = carry
            for p in range(pieces):
                cut = slice(p * size, (p + 1) * size)
                direction, image = dirs[k, :, cut], images[k, :, cut]
                product = part[k, :, cut]
                with_residual = with_residual + lanes(product * (direction - step * image))
                with_direction = with_direction + lanes(product * direction)
            return with_residual, with_direction

        return lax.fori_loop(0, n, body, carry)

    zero = jnp.zeros((fields, 128), F32)
    carry = over(sr, vr, wr, sr.shape[0], (zero, zero))
    return over(sc, vc, wc, sc.shape[0], carry)


def final_kernel(d, w, sr, sc, dots, vr, vc, wr, wc, x, res, sums, *rest):
    land, hold = rest[:7], rest[7:12]
    mine, land_a, land_b, csem, dsem = rest[12:]
    r, c, nr, nc = position()
    norm = jnp.sum(dots[0], axis=1, keepdims=True)
    cross = jnp.sum(dots[1], axis=1, keepdims=True)
    step = norm / cross
    residual = d[...] - step * w[...]
    barrier()
    parts = collect(sr, sc, sums, land, hold, csem)
    next(parts)
    with_residual, with_direction = local_dots(sr, sc, vr, vc, wr, wc, step)
    along = lanes(residual * w[...])
    mine[0, 0] = lanes(residual * residual)
    mine[0, 1] = along - step * (along + with_residual)
    mine[0, 2] = along - step * with_direction
    first = reduce_row(mine.at[0], land_a, dsem, 0)
    next(parts)
    finish(first)
    mine[1] = total_of(mine.at[0], land_a, nc - 1)
    second = reduce_col(mine.at[1], land_b, dsem, nc - 1)
    for _ in parts:
        pass
    finish(second)
    totals = total_of(mine.at[1], land_b, nr - 1)
    fresh = jnp.sum(totals[0], axis=1, keepdims=True)
    growth = fresh / norm
    square = jnp.sum(totals[1], axis=1, keepdims=True)
    mixed = jnp.sum(totals[2], axis=1, keepdims=True) + (cross - step * cross)
    stride = fresh / (square + growth * mixed + growth * growth * cross)
    image = w[...] + sums[...]
    direction = residual + growth * d[...]
    applied = w[...] - step * image + growth * w[...]
    x[...] = step * d[...] + stride * direction
    res[...] = residual - stride * applied


def params(cid=None):
    if cid is None:
        return pltpu.CompilerParams(vmem_limit_bytes=24000 * 1024)
    return pltpu.CompilerParams(collective_id=cid, has_side_effects=True, vmem_limit_bytes=24000 * 1024)


def shape(*dims, dtype=F32):
    return jax.ShapeDtypeStruct(dims, dtype)


def local(points, values, tile_lists):
    nr, nc = lax.axis_size("row"), lax.axis_size("col")
    fields, owned = values.shape
    slots = tile_lists.shape[1]
    peers = nr + nc - 2
    sem = lambda n: pltpu.SemaphoreType.DMA((2, n))
    rows, cols = shape(nc, fields, owned), shape(nr, fields, owned)
    tile = shape(slots, BLK, BLK, dtype=BF16)
    part = owned // 2
    landing = [
        pltpu.VMEM((fields, owned), F32),
        pltpu.VMEM((2, SIDE, 2, HALF, part), F32),
        pltpu.VMEM((2, SIDE, 2, HALF, owned), F32),
        pltpu.VMEM((2, 2, HALF, part), F32),
        pltpu.VMEM((2, 2, HALF, owned), F32),
        pltpu.VMEM((SIDE, fields, owned), F32),
        pltpu.VMEM((2, HALF, owned), F32),
        pltpu.VMEM((2, fields, owned), F32),
        pltpu.VMEM((2, SIDE, 2, HALF, owned), F32),
        pltpu.VMEM((2, SIDE, HALF, owned), F32),
        pltpu.VMEM((2, 2, HALF, owned), F32),
        pltpu.VMEM((SIDE, fields, owned), F32),
        pltpu.VMEM((2, fields, owned), F32),
    ]
    ways = 48

    khi, klo, vr, vc = pl.pallas_call(
        tiles_kernel,
        out_shape=(tile, tile, rows, cols),
        in_specs=[SM, VM, VM],
        out_specs=[VM] * 4,
        scratch_shapes=[
            pltpu.VMEM((owned // BLK, 3, BLK), F32),
            pltpu.VMEM((nc * owned // BLK, 3, BLK), F32),
            pltpu.VMEM((nr * owned // BLK, 3, BLK), F32),
            sem(peers), sem(ways),
        ],
        compiler_params=params(0),
        name="gather_and_tiles",
    )(tile_lists, points, values)

    apply = pl.pallas_call(
        apply_kernel,
        out_shape=(rows, cols),
        in_specs=[SM, VM, VM, VM, VM],
        out_specs=[VM] * 2,
        compiler_params=params(),
        name="apply_tiles",
    )
    sr, sc = apply(tile_lists, khi, klo, vr, vc)

    w, wr, wc, dots = pl.pallas_call(
        merge_kernel,
        out_shape=(shape(fields, owned), rows, cols, shape(2, fields, 128)),
        in_specs=[VM] * 5,
        out_specs=[VM] * 4,
        scratch_shapes=landing + [
            pltpu.VMEM((2, 2, fields, 128), F32),
            pltpu.VMEM((nc - 1, 2, fields, 128), F32),
            pltpu.VMEM((nr - 1, 2, fields, 128), F32),
            sem(ways), sem(ways), sem(peers),
        ],
        compiler_params=params(1),
        name="reduce_and_gather",
    )(values, sr, sc, vr, vc)

    sr, sc = apply(tile_lists, khi, klo, wr, wc)

    x, res = pl.pallas_call(
        final_kernel,
        out_shape=(shape(fields, owned), shape(fields, owned)),
        in_specs=[VM] * 9,
        out_specs=[VM] * 2,
        scratch_shapes=landing + [
            pltpu.VMEM((2, 3, fields, 128), F32),
            pltpu.VMEM((nc - 1, 3, fields, 128), F32),
            pltpu.VMEM((nr - 1, 3, fields, 128), F32),
            sem(ways), sem(peers),
        ],
        compiler_params=params(2),
        name="reduce_and_finish",
    )(values, w, sr, sc, dots, vr, vc, wr, wc)
    return x, res


def solution(mesh):
    placed = P(None, ("row", "col"))
    return jax.shard_map(
        local, mesh=mesh, in_specs=(placed,) * 3, out_specs=(placed, placed), check_vma=False
    )
```
